512 devices in a mesh: ens: 4 (over y_lo), oy: 32 (over y_hi, z, core), ox: 4 (over x).
Axes of the slice: x: 4, y: 8 (y_hi: 2, y_lo: 4; y = y_hi * 4 + y_lo), z: 8, core: 2. Of those that a mesh axis runs over, the one named last changes fastest.
Arguments:
- state: bfloat16 [4, 128, 512, 256], P('ens', 'oy', 'ox'), may hold values from -6 to 6
- state_cot: bfloat16 [4, 128, 512, 256], P('ens', 'oy', 'ox'), may hold values from -6 to 6
- flux_cot: bfloat16 [4, 8192, 4, 128], P('ens', ('oy', 'ox')), may hold values from -6 to 6
- conv_weight: bfloat16 [9, 256, 256], replicated, may hold values from -0.125 to 0.125
- mix_weight: bfloat16 [256, 256], replicated, may hold values from -0.375 to 0.375
- flux_weight: bfloat16 [4, 256], replicated, may hold values from -3 to 3
- regrid_weights: bfloat16 [16, 128, 128], replicated, may hold values from -0.5 to 0.5
- intersection_atm: int32 [128, 4, 4], replicated, may hold values from 0 to 8191, as said below
- intersection_offset: int32 [128, 4, 4], replicated, may hold values from 0 to 15
- wet_rows: int32 [32, 4], P('oy', 'ox'), may hold values from 1 to 4
Outputs:
- input_grad: bfloat16 [4, 128, 512, 256], P('ens', 'oy', 'ox')
- weight_grads: float32 [2560, 256], P(('oy', 'ox'))
- flux_grad: float32 [4, 256], replicated
The draws below stay inside these ranges and needn't reach their ends.
Inputs may be any that keep to these rules, and one draw needn't show every extreme that they name: `intersection_atm`: atmosphere block a lies on device a // 64, numbered oy 4 + ox. The intersections of the ocean blocks of device (oy, ox), that is of latitude rows oy 4 to oy 4 + 3 and longitude block ox, lie on exactly four atmosphere devices, two with index oy and two with index (oy + 1) mod 32 along oy. At most 5 of that device's 4 x 4 intersections lie on one atmosphere device, and for every ocean device exactly 5 lie on one of them.
All inputs are finite; a program needn't handle non-finite values.
Results may differ from the reference program's by a relative error of at most 0.0085.
Values may be sent and summed in bfloat16 or wider, within the bound.
No kernel may reach another device: no remote copies, remote signals or barrier semaphores. Data moves between devices by JAX's collectives and lax.ppermute only.
A program may use at most 64 MiB of HBM per device.

```python
import math
import jax
import jax.numpy as jnp
from jax import lax

C = 256
BLOCK = 128
FLUX = 4
INTERSECTIONS = 4
ROWS_DEV = 4
ATM_DEV = 64
NMAT = 16
CAP = 5
LAT_TILES = 32
LON_BLOCKS = 4
MEMBERS = 4
NLAT = 128
NLON = 512
ATM_BLOCKS = 8192


def draw_intersection_atm(key, part):
    device_count = LAT_TILES * LON_BLOCKS
    entries = ROWS_DEV * INTERSECTIONS

    def draw_device(dev_index):
        dev_key = jax.random.fold_in(jax.random.fold_in(key, 7301), dev_index)
        key_rest, key_mix, key_corner, key_first, key_second, key_local = jax.random.split(dev_key, 6)
        pool_index = jax.random.permutation(key_rest, 3 * CAP - 3)[:entries - CAP - 3]
        pool_group = 1 + pool_index // (CAP - 1)
        pool_slot = pool_group * CAP + 1 + pool_index % (CAP - 1)
        firsts = jnp.arange(1, 4) * CAP
        chosen = jnp.concatenate([jnp.arange(CAP), firsts, pool_slot])
        chosen = jax.random.permutation(key_mix, chosen)
        owner_slot = chosen // CAP
        corner_order = jax.random.permutation(key_corner, 4)
        corner = corner_order[owner_slot]
        cols_first = jax.random.permutation(key_first, LON_BLOCKS)[:2]
        cols_second = jax.random.permutation(key_second, LON_BLOCKS)[:2]
        dev_row = dev_index // LON_BLOCKS
        owner_row = (dev_row + corner // 2) % LAT_TILES
        owner_col = jnp.where(corner // 2 == 0, cols_first[corner % 2], cols_second[corner % 2])
        local_block = jax.random.randint(key_local, (entries,), 0, ATM_DEV)
        return (owner_row * LON_BLOCKS + owner_col) * ATM_DEV + local_block
    owner_table = jax.vmap(draw_device)(jnp.arange(device_count))
    owner_table = owner_table.reshape(LAT_TILES, LON_BLOCKS, ROWS_DEV, INTERSECTIONS).transpose(0, 2, 1, 3)
    return owner_table.reshape(LAT_TILES * ROWS_DEV, LON_BLOCKS, INTERSECTIONS).astype(jnp.int32)


def with_ends(values, rng, least, high):
    longest = values.shape.index(max(values.shape))
    spots = []
    for shift in (0, 1):
        where = [jax.random.randint(jax.random.fold_in(rng, axis), (), 0, length) for axis, length in enumerate(values.shape)]
        where[longest] = (where[longest] + shift) % values.shape[longest]
        spots.append(tuple(where))
    return values.at[spots[0]].set(least).at[spots[1]].set(high)


def block_scale(key, extent, cuts, low, largest):
    level, own = 1.0, jax.random.fold_in(key, 6)
    for axis_at, blocks in cuts:
        steps = jnp.exp(jax.random.uniform(jax.random.fold_in(own, axis_at), (blocks,), jnp.float32, low / len(cuts), largest / len(cuts)))
        level = level * jnp.repeat(steps, extent[axis_at] // blocks).reshape([-1 if axis == axis_at else 1 for axis in range(len(extent))])
    return level


def centred(stream_key, extent, deviation, limit, cuts=(), dtype=jnp.bfloat16):
    drawn = jax.random.normal(stream_key, extent, jnp.float32) * deviation
    if len(cuts) > 0:
        drawn = block_scale(stream_key, extent, cuts, -0.22, 0.18) * drawn
    return jnp.clip(drawn, min=-limit, max=limit).astype(dtype)


def setup_inputs(seed: int = 0) -> dict:
    arg_keys = jax.random.split(jax.random.key(seed), 11)
    state = centred(arg_keys[0], (MEMBERS, NLAT, NLON, C), 1.0, 6.0, ((0, 4), (1, 32), (2, 4)))
    state_cot = centred(arg_keys[1], (MEMBERS, NLAT, NLON, C), 1.0, 6.0, ((0, 4), (1, 32), (2, 4)))
    flux_cot = centred(arg_keys[2], (MEMBERS, ATM_BLOCKS, FLUX, BLOCK), 1.0, 6.0, ((0, 4), (1, 128)))
    conv_weight = centred(arg_keys[3], (9, C, C), (9 * C) ** -0.5, 0.125)
    mix_weight = centred(arg_keys[4], (C, C), C ** -0.5, 0.375)
    flux_weight = centred(arg_keys[5], (FLUX, C), 0.5, 3.0)
    regrid_weights = centred(arg_keys[6], (NMAT, BLOCK, BLOCK), BLOCK ** -0.5, 0.5)
    intersection_atm = draw_intersection_atm(jax.random.fold_in(arg_keys[10], 71), 0)
    intersection_offset = with_ends(jax.random.randint(arg_keys[8], (NLAT, LON_BLOCKS, INTERSECTIONS), 0, NMAT), jax.random.fold_in(arg_keys[8], 1), 0, NMAT - 1).astype(jnp.int32)
    wet_rows = with_ends(jax.random.randint(arg_keys[9], (LAT_TILES, LON_BLOCKS), 1, ROWS_DEV + 1), jax.random.fold_in(arg_keys[9], 1), 1, ROWS_DEV).astype(jnp.int32)
    return {"state": state, "state_cot": state_cot, "flux_cot": flux_cot, "conv_weight": conv_weight, "mix_weight": mix_weight, "flux_weight": flux_weight, "regrid_weights": regrid_weights, "intersection_atm": intersection_atm, "intersection_offset": intersection_offset, "wet_rows": wet_rows}


def rim_pad(field):
    padded = jnp.pad(field, ((1, 1), (0, 0), (0, 0)))
    return jnp.concatenate([padded[:, -1:], padded, padded[:, :1]], axis=1)

def one_member(tile_state, tile_cot, member_flux, conv_weight, mix_weight, flux_weight, regrid_weights, intersection_atm, intersection_offset, wet_mask):
    lat_rows, lon_cells, channels = tile_state.shape
    padded = rim_pad(tile_state)
    hidden = jnp.zeros((lat_rows * lon_cells, channels), jnp.float32)
    for tap_index in range(9):
        tap_row, tap_col = (tap_index // 3, tap_index % 3)
        patch_rows = padded[tap_row:tap_row + lat_rows, tap_col:tap_col + lon_cells].reshape(-1, channels)
        hidden = hidden + jnp.dot(patch_rows, conv_weight[tap_index], preferred_element_type=jnp.float32)
    activation = jax.nn.silu(hidden).astype(jnp.bfloat16)
    flux_cells = jnp.zeros((lat_rows, LON_BLOCKS, FLUX, BLOCK), jnp.float32)
    for intersection in range(INTERSECTIONS):
        picked_cot = member_flux[intersection_atm[:, :, intersection]].astype(jnp.float32)
        picked_maps = regrid_weights[intersection_offset[:, :, intersection]].astype(jnp.float32)
        contribution = jnp.einsum('ijfa,ijoa->ijfo', picked_cot, picked_maps).astype(jnp.bfloat16)
        contribution = lax.optimization_barrier(contribution)
        flux_cells = flux_cells + contribution.astype(jnp.float32)
    flux_cells = flux_cells * wet_mask[:, :, None, None]
    cot_flat = tile_cot.reshape(-1, channels)
    act_grad = lax.dot_general(cot_flat, mix_weight, (((1,), (1,)), ((), ())), preferred_element_type=jnp.float32)
    act_grad = act_grad + jnp.einsum('ijfb,fc->ijbc', flux_cells, flux_weight.astype(jnp.float32)).reshape(-1, channels)
    gate_sig = jax.nn.sigmoid(hidden)
    hidden_grad = (act_grad * gate_sig * (1.0 + hidden * (1.0 - gate_sig))).astype(jnp.bfloat16)
    padded_grad = rim_pad(hidden_grad.reshape(lat_rows, lon_cells, channels))
    input_grad = cot_flat.astype(jnp.float32)
    tap_grads = []
    for tap_index in range(9):
        tap_row, tap_col = (tap_index // 3, tap_index % 3)
        back_rows = padded_grad[2 - tap_row:2 - tap_row + lat_rows, 2 - tap_col:2 - tap_col + lon_cells].reshape(-1, channels)
        input_grad = input_grad + lax.dot_general(back_rows, conv_weight[tap_index], (((1,), (1,)), ((), ())), preferred_element_type=jnp.float32)
        patch_rows = padded[tap_row:tap_row + lat_rows, tap_col:tap_col + lon_cells].reshape(-1, channels)
        tap_grads.append(lax.dot_general(patch_rows, hidden_grad, (((0,), (0,)), ((), ())), preferred_element_type=jnp.float32))
    tap_grads.append(lax.dot_general(activation, cot_flat, (((0,), (0,)), ((), ())), preferred_element_type=jnp.float32))
    weight_term = jnp.concatenate(tap_grads, axis=0)
    flux_term = jnp.einsum('ijfb,ijbc->fc', flux_cells, activation.reshape(lat_rows, LON_BLOCKS, BLOCK, channels).astype(jnp.float32))
    return (input_grad.reshape(lat_rows, lon_cells, channels).astype(jnp.bfloat16), weight_term, flux_term)

def reference(state, state_cot, flux_cot, conv_weight, mix_weight, flux_weight, regrid_weights, intersection_atm, intersection_offset, wet_rows):
    row_local = jnp.arange(NLAT).astype(jnp.int32) % ROWS_DEV
    wet_counts = jnp.repeat(wet_rows, ROWS_DEV, axis=0)
    wet_mask = (row_local[:, None] < wet_counts).astype(jnp.float32)

    def member_step(inputs):
        return one_member(inputs[0], inputs[1], inputs[2], conv_weight, mix_weight, flux_weight, regrid_weights, intersection_atm, intersection_offset, wet_mask)
    input_grad, weight_terms, flux_terms = lax.map(member_step, (state, state_cot, flux_cot))
    grad_scale = 1.0 / math.sqrt(MEMBERS * NLAT * NLON)
    weight_grads = lax.optimization_barrier(jnp.sum(weight_terms, axis=0)) * grad_scale
    flux_grad = lax.optimization_barrier(jnp.sum(flux_terms, axis=0)) * grad_scale
    return (input_grad, weight_grads, flux_grad)
```

```python
import math

import jax
import jax.numpy as jnp
from jax import lax
from jax.experimental import pallas as pl
from jax.experimental.pallas import tpu as pltpu
from jax.sharding import Mesh, PartitionSpec as P

BF = jnp.bfloat16
F32 = jnp.float32
OY = ("yh", "z", "core")
ROWS = 4
CELLS = 128
CH = 256
NLON = 4
ENTRIES = 16
SHARE = 20
VM = pl.BlockSpec(memory_space=pltpu.VMEM)
SM = pl.BlockSpec(memory_space=pltpu.SMEM)


def oy_index():
    return lax.axis_index("yh") * 16 + lax.axis_index("z") * 2 + lax.axis_index("core")


def call(kernel, outs, scratch=(), specs=None, n_in=None):
    return pl.pallas_call(
        kernel,
        out_shape=outs,
        in_specs=specs if specs is not None else [VM] * n_in,
        out_specs=jax.tree.map(lambda _: VM, outs),
        scratch_shapes=list(scratch),
    )


def struct(shape, dtype):
    return jax.ShapeDtypeStruct(shape, dtype)


def split_two(value):
    high = value.astype(BF)
    low = (value - high.astype(F32)).astype(BF)
    return high, low


def dot(a, b, dims):
    return lax.dot_general(a, b, (dims, ((), ())), preferred_element_type=F32)


def edge_rows(mid, above, below, edge):
    at = 0 if edge == 0 else 15
    base = 0 if edge == 0 else CELLS - 16
    rows = [above[base : base + 16, :].astype(F32)[at : at + 1]]
    for r in range(ROWS):
        rows.append(mid[r * CELLS + base : r * CELLS + base + 16, :].astype(F32)[at : at + 1])
    rows.append(below[base : base + 16, :].astype(F32)[at : at + 1])
    rows.append(jnp.zeros((2, CH), F32))
    return jnp.concatenate(rows, axis=0)


def pack_kernel(iatm, state, below, above, flux_own, out):
    oy = oy_index()
    ox = lax.axis_index("ox")
    me = (oy * NLON + ox) * 64
    nxt = (lax.rem(oy + 1, 32) * NLON + ox) * 64
    row = lax.broadcasted_iota(jnp.int32, (64, 128), 0)
    lane = lax.broadcasted_iota(jnp.int32, (64, 128), 1)
    target = jnp.zeros((64, 128), jnp.int32)
    for d in range(NLON):
        for r in range(ROWS):
            for k in range(4):
                value = iatm[((oy * ROWS + r) * NLON + d) * 4 + k]
                target = jnp.where(row == d * 16 + r * 4 + k, value, target)
    wanted = jnp.where(lane < 64, lane + me, lane - 64 + nxt)
    pick = jnp.where(target == wanted, 1.0, 0.0).astype(BF)
    for h in range(2):
        source = jnp.concatenate(
            [flux_own[h * 64 : h * 64 + 64, :], below[128 + h * 64 : 192 + h * 64, :]], axis=0
        )
        got = dot(pick, source, ((1,), (0,))).astype(BF)
        for d in range(NLON):
            out[d, h * 16 : h * 16 + 16, :] = got[d * 16 : d * 16 + 16]
    top_keep = jnp.where(oy > 0, 1.0, 0.0)
    bottom_keep = jnp.where(oy < 31, 1.0, 0.0)
    part = lax.broadcasted_iota(jnp.int32, (8, CH), 0)
    keep = jnp.where(part == 0, top_keep, jnp.where(part == ROWS + 1, bottom_keep, 1.0))
    first = edge_rows(state, above, below, 0) * keep
    last = edge_rows(state, above, below, 1) * keep
    for d in range(NLON):
        to_right = jnp.where(lax.rem(ox + 1, NLON) == d, 1.0, 0.0)
        to_left = jnp.where(lax.rem(ox + NLON - 1, NLON) == d, 1.0, 0.0)
        halo = last * to_right + first * to_left
        out[d, 32:48, :] = jnp.concatenate([halo, jnp.zeros((8, CH), F32)], axis=0).astype(BF)


def build_shifts(shifted, mid, above, below, left, right, top_keep, bottom_keep):
    cell = lax.broadcasted_iota(jnp.int32, (CELLS, CH), 0)
    for r in range(ROWS + 2):
        if r == 0:
            value = above[0:CELLS, :].astype(F32) * top_keep
        elif r == ROWS + 1:
            value = below[0:CELLS, :].astype(F32) * bottom_keep
        else:
            value = mid[(r - 1) * CELLS : r * CELLS, :].astype(F32)
        shifted[1, r * CELLS : (r + 1) * CELLS, :] = value.astype(BF)
        plus = jnp.where(cell == CELLS - 1, right[r : r + 1, :], pltpu.roll(value, CELLS - 1, 0))
        minus = jnp.where(cell == 0, left[r : r + 1, :], pltpu.roll(value, 1, 0))
        shifted[2, r * CELLS : (r + 1) * CELLS, :] = plus.astype(BF)
        shifted[0, r * CELLS : (r + 1) * CELLS, :] = minus.astype(BF)


def main_kernel(
    ioff,
    wet,
    state,
    below,
    above,
    arrived,
    cot,
    conv,
    mix,
    flux_weight,
    regrid,
    hg_out,
    send_out,
    keep_out,
    zrow_out,
    shifted,
    turned,
    hidden,
    grads,
):
    oy = oy_index()
    ox = lax.axis_index("ox")
    core = lax.axis_index("core")
    top_keep = jnp.where(oy > 0, 1.0, 0.0)
    bottom_keep = jnp.where(oy < 31, 1.0, 0.0)
    left = arrived[lax.rem(ox + NLON - 1, NLON), 32:48, :].astype(F32)
    right = arrived[lax.rem(ox + 1, NLON), 32:48, :].astype(F32)
    build_shifts(shifted, state, above, below, left, right, top_keep, bottom_keep)
    for half in range(2):
        acc = jnp.zeros((256, CH), F32)
        for t in range(9):
            start = (t // 3) * CELLS + half * 256
            acc = acc + dot(shifted[t % 3, start : start + 256, :], conv[t], ((1,), (0,)))
        hidden[half * 256 : half * 256 + 256, :] = acc
    flux = [
        sum(arrived[s, h * 16 : h * 16 + 16, :].astype(F32) for s in range(NLON)) for h in range(2)
    ]
    blocks = jnp.concatenate(
        [flux[f // 2][:, (f % 2) * 128 : (f % 2) * 128 + 128] for f in range(4)], axis=0
    ).astype(BF)
    row = lax.broadcasted_iota(jnp.int32, (64, 128), 0)
    offset = jnp.zeros((64, 128), jnp.int32)
    for r in range(ROWS):
        for k in range(4):
            value = ioff[((oy * ROWS + r) * NLON + ox) * 4 + k]
            offset = jnp.where(lax.rem(row, 16) == r * 4 + k, value, offset)
    contribution = jnp.zeros((64, 128), F32)
    for m in range(16):
        product = dot(blocks, regrid[m], ((1,), (1,)))
        contribution = jnp.where(offset == m, product, contribution)
    contribution = contribution.astype(BF)
    out_row = lax.broadcasted_iota(jnp.int32, (16, 64), 0)
    in_row = lax.broadcasted_iota(jnp.int32, (16, 64), 1)
    same_field = lax.rem(out_row, 4) == in_row // 16
    same_row = out_row // 4 == lax.rem(in_row, 16) // 4
    is_wet = out_row // 4 < wet[0, 0]
    gather = jnp.where(
        jnp.logical_and(jnp.logical_and(same_field, same_row), is_wet), 1.0, 0.0
    ).astype(BF)
    cells = dot(gather, contribution, ((1,), (0,)))
    cells_high, cells_low = split_two(cells)
    cells_pair = jnp.concatenate([cells_high, cells_low], axis=0)
    pair_row = lax.broadcasted_iota(jnp.int32, (32, CH), 0)
    field_weights = jnp.concatenate([flux_weight[...].astype(F32)] * 8, axis=0)
    flux_part = jnp.zeros((32, CH), F32)
    for r in range(ROWS):
        lo, hi = r * CELLS, (r + 1) * CELLS
        mine = lax.rem(pair_row, 16) // 4 == r
        weights = jnp.where(mine, field_weights, 0.0).astype(BF)
        act_grad = dot(cot[lo:hi, :], mix[...], ((1,), (1,)))
        act_grad = act_grad + dot(cells_pair, weights, ((0,), (0,)))
        value = hidden[lo:hi, :]
        gate = jax.nn.sigmoid(value)
        activation = (value * gate).astype(BF)
        grad = (act_grad * gate * (1.0 + value * (1.0 - gate))).astype(BF)
        hg_out[lo:hi, :] = grad
        turned[3, :, lo:hi] = activation.T
        flux_part = flux_part + jnp.where(
            mine, dot(cells_pair, activation, ((1,), (0,))), 0.0
        )
    scale = 1.0 / 512.0
    flux_total = jnp.zeros((4, CH), F32)
    for part in range(8):
        flux_total = flux_total + flux_part[part * 4 : part * 4 + 4]
    flux_high, flux_low = split_two(flux_total * scale)
    flux_rows = jnp.concatenate([flux_high.astype(F32), flux_low.astype(F32)], axis=0)
    for q in range(3):
        turned[q] = shifted[q].T
    for t in range(9):
        start = (t // 3) * CELLS
        product = dot(turned[t % 3, :, start : start + 512], hg_out[...], ((1,), (0,)))
        grads[t * CH : (t + 1) * CH, :] = product * scale
    product = dot(turned[3, :, 0:512], cot[...], ((1,), (0,)))
    grads[9 * CH : 10 * CH, :] = product * scale
    for m in range(16):
        mine = pl.multiple_of(m * 160 + core * 80, 8)
        other = pl.multiple_of(m * 160 + 80 - core * 80, 8)
        keep_out[m * 80 : m * 80 + 80, :] = grads[pl.ds(mine, 80), :]
        send_out[m * 80 : m * 80 + 80, :] = grads[pl.ds(other, 80), :].astype(BF)
    keep_out[1280:1288, :] = flux_rows
    send_out[1280:1296, :] = jnp.concatenate(
        [flux_rows, jnp.zeros((8, CH), F32)], axis=0
    ).astype(BF)
    first, last = hg_out[0:CELLS, :], hg_out[3 * CELLS : 4 * CELLS, :]
    send_out[1296:1424, :] = jnp.where(core == 0, last, first)
    zrow_out[...] = jnp.where(core == 0, first, last)


def merge_kernel(keep, got, zrow, hg, out, rows_out, total, moved):
    oy = oy_index()
    ox = lax.axis_index("ox")
    core = lax.axis_index("core")
    total[...] = keep[0:1280, :] + got[0:1280, :].astype(F32)
    for c in range(NLON):
        for z in range(8):
            for yh in range(2):
                m = yh * 8 + z
                to = c * 320 + (z * 2 + yh) * SHARE
                moved[to : to + SHARE, :] = total[m * 80 + c * SHARE : m * 80 + c * SHARE + SHARE, :]
    flux = keep[1280:1288, :] + got[1280:1296, :].astype(F32)[0:8]
    flux_high, flux_low = split_two(flux[0:4] + flux[4:8])
    top_keep = jnp.where(oy > 0, 1.0, 0.0)
    bottom_keep = jnp.where(oy < 31, 1.0, 0.0)
    inside = got[1296:1424, :].astype(F32)
    across = zrow[...].astype(F32)
    above = (jnp.where(core == 0, across, inside) * top_keep).astype(BF)
    below = (jnp.where(core == 0, inside, across) * bottom_keep).astype(BF)
    rows_out[0:CELLS, :] = above
    rows_out[CELLS : 2 * CELLS, :] = below
    first = edge_rows(hg, above, below, 0)
    last = edge_rows(hg, above, below, 1)
    for c in range(NLON):
        to_right = jnp.where(lax.rem(ox + 1, NLON) == c, 1.0, 0.0)
        to_left = jnp.where(lax.rem(ox + NLON - 1, NLON) == c, 1.0, 0.0)
        halo = last * to_right + first * to_left
        out[c, 0:320, :] = moved[c * 320 : c * 320 + 320, :].astype(BF)
        out[c, 320:336, :] = jnp.concatenate(
            [flux_high.astype(F32), flux_low.astype(F32), halo], axis=0
        ).astype(BF)


def sum_flux(pieces):
    total = pieces[0]
    for piece in pieces[1:]:
        total = total + piece
    return total[0:4] + total[4:8]


def ox_sum_kernel(got, out):
    for z in range(8):
        piece = got[0, z * 40 : z * 40 + 40, :].astype(F32)
        for s in range(1, NLON):
            piece = piece + got[s, z * 40 : z * 40 + 40, :].astype(F32)
        out[z, 0:40, :] = piece.astype(BF)
    flux = sum_flux([got[s, 320:336, :].astype(F32)[0:8] for s in range(NLON)])
    high, low = split_two(flux)
    rows = jnp.concatenate([high.astype(F32), low.astype(F32)], axis=0).astype(BF)
    for z in range(8):
        out[z, 40:48, :] = rows


def z_sum_kernel(got, out):
    piece = got[0].astype(F32)
    for s in range(1, 8):
        piece = piece + got[s].astype(F32)
    high, low = split_two(piece[40:44] + piece[44:48])
    flux = jnp.concatenate([high.astype(F32), low.astype(F32)], axis=0)
    pad = jnp.zeros((4, CH), F32)
    for yh in range(2):
        rows = jnp.concatenate([piece[yh * SHARE : yh * SHARE + SHARE], pad, flux], axis=0).astype(BF)
        for e in range(4):
            out[e * 2 + yh] = rows


def last_sum_kernel(got, weight_out, flux_out):
    piece = got[0].astype(F32)
    for s in range(1, 8):
        piece = piece + got[s].astype(F32)
    weight_out[...] = piece[0:SHARE]
    flux_out[...] = piece[24:28] + piece[28:32]


def input_kernel(hg, rows, arrived, cot, conv, out, shifted):
    ox = lax.axis_index("ox")
    left = arrived[lax.rem(ox + NLON - 1, NLON), 320:336, :].astype(F32)[8:16]
    right = arrived[lax.rem(ox + 1, NLON), 320:336, :].astype(F32)[8:16]
    build_shifts(
        shifted, hg, rows, rows.at[CELLS : 2 * CELLS, :], left, right, 1.0, 1.0
    )
    for half in range(2):
        acc = cot[half * 256 : half * 256 + 256, :].astype(F32)
        for t in range(9):
            start = (2 - t // 3) * CELLS + half * 256
            acc = acc + dot(shifted[2 - t % 3, start : start + 256, :], conv[t], ((1,), (1,)))
        out[half * 256 : half * 256 + 256, :] = acc.astype(BF)


def body(
    state,
    state_cot,
    flux_cot,
    conv_weight,
    mix_weight,
    flux_weight,
    regrid_weights,
    intersection_atm,
    intersection_offset,
    wet_rows,
):
    state = state.reshape(ROWS * CELLS, CH)
    cot = state_cot.reshape(ROWS * CELLS, CH)
    flux_own = (
        flux_cot.reshape(64, 2, CH).transpose(1, 0, 2).reshape(128, CH)
    )
    iatm = intersection_atm.reshape(-1)
    ioff = intersection_offset.reshape(-1)
    up = jnp.concatenate([state[0:CELLS], flux_own], axis=0)
    below = lax.ppermute(up, OY, [((i + 1) % 32, i) for i in range(32)])
    above = lax.ppermute(state[3 * CELLS :], OY, [(i, (i + 1) % 32) for i in range(32)])
    packed = call(
        pack_kernel, struct((NLON, 48, CH), BF), specs=[SM] + [VM] * 4
    )(iatm, state, below, above, flux_own)
    arrived = lax.all_to_all(packed, "ox", 0, 0, tiled=True)
    hg, send, keep, zrow = call(
        main_kernel,
        (
            struct((ROWS * CELLS, CH), BF),
            struct((1424, CH), BF),
            struct((1288, CH), F32),
            struct((CELLS, CH), BF),
        ),
        scratch=[
            pltpu.VMEM((3, 768, CH), BF),
            pltpu.VMEM((4, CH, 768), BF),
            pltpu.VMEM((512, CH), F32),
            pltpu.VMEM((2560, CH), F32),
        ],
        specs=[SM, SM] + [VM] * 9,
    )(ioff, wet_rows, state, below, above, arrived, cot, conv_weight, mix_weight, flux_weight, regrid_weights)
    zgot = lax.ppermute(zrow, OY, [(i, (i - 1) % 32 if i % 2 == 0 else (i + 1) % 32) for i in range(32)])
    got = lax.ppermute(send, "core", [(0, 1), (1, 0)])
    packed, rows = call(
        merge_kernel,
        (struct((NLON, 336, CH), BF), struct((2 * CELLS, CH), BF)),
        scratch=[pltpu.VMEM((1280, CH), F32), pltpu.VMEM((1280, CH), F32)],
        n_in=4,
    )(keep, got, zgot, hg)
    by_ox = lax.all_to_all(packed, "ox", 0, 0, tiled=True)
    packed = call(ox_sum_kernel, struct((8, 48, CH), BF), n_in=1)(by_ox)
    by_z = lax.all_to_all(packed, "z", 0, 0, tiled=True)
    packed = call(z_sum_kernel, struct((8, 32, CH), BF), n_in=1)(by_z)
    by_rest = lax.all_to_all(packed, ("ens", "yh"), 0, 0, tiled=True)
    weight_out, flux_out = call(
        last_sum_kernel, (struct((SHARE, CH), F32), struct((4, CH), F32)), n_in=1
    )(by_rest)
    input_grad = call(
        input_kernel,
        struct((ROWS * CELLS, CH), BF),
        scratch=[pltpu.VMEM((3, 768, CH), BF)],
        n_in=5,
    )(hg, rows, by_ox, cot, conv_weight)
    return (input_grad.reshape(1, ROWS, CELLS, CH), weight_out, flux_out)


def solution(mesh):
    fine = Mesh(mesh.devices.reshape(4, 2, 8, 2, 4), ("ens", "yh", "z", "core", "ox"))
    in_specs = (
        P("ens", OY, "ox", None),
        P("ens", OY, "ox", None),
        P("ens", OY + ("ox",), None, None),
        P(),
        P(),
        P(),
        P(),
        P(),
        P(),
        P(OY, "ox"),
    )
    out_specs = (P("ens", OY, "ox", None), P(OY + ("ox",), None), P())
    return jax.shard_map(body, mesh=fine, in_specs=in_specs, out_specs=out_specs, check_vma=False)
```

```python
import math

import jax
import jax.numpy as jnp
from jax import lax
from jax.experimental import pallas as pl
from jax.experimental.pallas import tpu as pltpu
from jax.sharding import Mesh, PartitionSpec as P

BF = jnp.bfloat16
F32 = jnp.float32
OY = ("yh", "z", "core")
ROWS = 4
CELLS = 128
CH = 256
NLON = 4
ENTRIES = 16
SHARE = 20
VM = pl.BlockSpec(memory_space=pltpu.VMEM)
HBM = pl.BlockSpec(memory_space=pltpu.HBM)
SM = pl.BlockSpec(memory_space=pltpu.SMEM)


def oy_index():
    return lax.axis_index("yh") * 16 + lax.axis_index("z") * 2 + lax.axis_index("core")


def call(kernel, outs, scratch=(), specs=None, n_in=None):
    specs = specs if specs is not None else [VM] * n_in
    run = pl.pallas_call(
        kernel,
        out_shape=outs,
        in_specs=specs,
        out_specs=jax.tree.map(lambda _: VM, outs),
        scratch_shapes=list(scratch),
        compiler_params=pltpu.CompilerParams(vmem_limit_bytes=24 << 20),
    )

    def placed(*args):
        return run(
            *[
                pltpu.with_memory_space_constraint(a, s.memory_space) if s is not SM else a
                for a, s in zip(args, specs)
            ]
        )

    return placed


def struct(shape, dtype):
    return pltpu.VMEM(shape, dtype)


def split_two(value):
    high = value.astype(BF)
    low = (value - high.astype(F32)).astype(BF)
    return high, low


def dot(a, b, dims):
    return lax.dot_general(a, b, (dims, ((), ())), preferred_element_type=F32)


def edge_cells(pieces, edge):
    at, base = (0, 0) if edge == 0 else (15, CELLS - 16)
    rows = []
    for piece in pieces:
        if piece is None:
            rows.append(jnp.zeros((1, CH), F32))
        else:
            rows.append(piece[base : base + 16, :].astype(F32)[at : at + 1])
    return jnp.concatenate(rows, axis=0)


def own_rows(ref):
    return [ref[r * CELLS : (r + 1) * CELLS, :] for r in range(ROWS)]


def joined(ref):
    return jnp.concatenate([ref[0:CELLS, :], ref[CELLS : 2 * CELLS, :]], axis=1)


def first_kernel(state_in, flux_in, up, down, state, flux, planes, sems):
    copies = [
        pltpu.make_async_copy(state_in, state, sems.at[0]),
        pltpu.make_async_copy(flux_in, flux, sems.at[1]),
    ]
    for copy in copies:
        copy.start()
    for copy in copies:
        copy.wait()
    up[0:CELLS, :] = state[0:CELLS, 0:128]
    up[CELLS : 2 * CELLS, :] = state[0:CELLS, 128:256]
    down[...] = state[3 * CELLS : 4 * CELLS, :]
    for b in range(64):
        block = flux[b].astype(F32)
        for f in range(4):
            planes[f * 64 + b : f * 64 + b + 1, :] = block[f : f + 1]
    up[2 * CELLS : 4 * CELLS, :] = planes[...].astype(BF)


def pick_kernel(iatm, ioff, *refs):
    sources, pick, offset_out, targets, sems = refs[:5], refs[5], refs[6], refs[7:12], refs[12]
    copies = [
        pltpu.make_async_copy(source, target, sems.at[n])
        for n, (source, target) in enumerate(zip(sources, targets))
    ]
    for copy in copies:
        copy.start()
    oy = oy_index()
    ox = lax.axis_index("ox")
    me = (oy * NLON + ox) * 64
    nxt = (lax.rem(oy + 1, 32) * NLON + ox) * 64
    row = lax.broadcasted_iota(jnp.int32, (64, 128), 0)
    lane = lax.broadcasted_iota(jnp.int32, (64, 128), 1)
    target = jnp.zeros((64, 128), jnp.int32)
    offset = jnp.zeros((64, 128), jnp.int32)
    for r in range(ROWS):
        for k in range(4):
            for d in range(NLON):
                value = iatm[((oy * ROWS + r) * NLON + d) * 4 + k]
                target = jnp.where(row == d * 16 + r * 4 + k, value, target)
            value = ioff[((oy * ROWS + r) * NLON + ox) * 4 + k]
            offset = jnp.where(lax.rem(row, 16) == r * 4 + k, value, offset)
    wanted = jnp.where(lane < 64, lane + me, lane - 64 + nxt)
    pick[...] = jnp.where(target == wanted, 1.0, 0.0).astype(BF)
    offset_out[...] = offset
    for copy in copies:
        copy.wait()


def pack_kernel(pick, state, below, above, up, out):
    oy = oy_index()
    ox = lax.axis_index("ox")
    for f in range(4):
        lo = 2 * CELLS + f * 64
        source = jnp.concatenate([up[lo : lo + 64, :], below[lo : lo + 64, :]], axis=0)
        got = dot(pick[...], source, ((1,), (0,))).astype(BF)
        for d in range(NLON):
            to = (f % 2) * 128
            out[d, (f // 2) * 16 : (f // 2) * 16 + 16, to : to + 128] = got[d * 16 : d * 16 + 16]
    top_keep = jnp.where(oy > 0, 1.0, 0.0)
    bottom_keep = jnp.where(oy < 31, 1.0, 0.0)
    part = lax.broadcasted_iota(jnp.int32, (6, CH), 0)
    keep = jnp.where(part == 0, top_keep, jnp.where(part == ROWS + 1, bottom_keep, 1.0))
    pieces = [above[...]] + own_rows(state) + [joined(below)]
    first = edge_cells(pieces, 0) * keep
    last = edge_cells(pieces, 1) * keep
    for d in range(NLON):
        to_right = jnp.where(lax.rem(ox + 1, NLON) == d, 1.0, 0.0)
        to_left = jnp.where(lax.rem(ox + NLON - 1, NLON) == d, 1.0, 0.0)
        halo = last * to_right + first * to_left
        out[d, 32:48, :] = jnp.concatenate([halo, jnp.zeros((10, CH), F32)], axis=0).astype(BF)


def build_shifts(shifted, pieces, left, right):
    cell = lax.broadcasted_iota(jnp.int32, (CELLS, CH), 0)
    for r, piece in enumerate(pieces):
        value = piece.astype(F32)
        shifted[1, r * CELLS : (r + 1) * CELLS, :] = piece.astype(BF)
        plus = jnp.where(cell == CELLS - 1, right[r : r + 1, :], pltpu.roll(value, CELLS - 1, 0))
        minus = jnp.where(cell == 0, left[r : r + 1, :], pltpu.roll(value, 1, 0))
        shifted[2, r * CELLS : (r + 1) * CELLS, :] = plus.astype(BF)
        shifted[0, r * CELLS : (r + 1) * CELLS, :] = minus.astype(BF)


def main_kernel(
    wet,
    offset,
    state,
    below,
    above,
    arrived,
    cot,
    conv,
    mix,
    flux_weight,
    regrid,
    hg_out,
    send_out,
    keep_out,
    zrow_out,
    shifted,
    turned,
    hidden,
    grads,
):
    oy = oy_index()
    ox = lax.axis_index("ox")
    core = lax.axis_index("core")
    top_keep = jnp.where(oy > 0, 1.0, 0.0)
    bottom_keep = jnp.where(oy < 31, 1.0, 0.0)
    left = arrived[lax.rem(ox + NLON - 1, NLON), 32:48, :].astype(F32)
    right = arrived[lax.rem(ox + 1, NLON), 32:48, :].astype(F32)
    top = above[...].astype(F32) * top_keep
    bottom = joined(below).astype(F32) * bottom_keep
    build_shifts(shifted, [top] + own_rows(state) + [bottom], left, right)
    for half in range(2):
        acc = jnp.zeros((256, CH), F32)
        for t in range(9):
            start = (t // 3) * CELLS + half * 256
            acc = acc + dot(shifted[t % 3, start : start + 256, :], conv[t], ((1,), (0,)))
        hidden[half * 256 : half * 256 + 256, :] = acc
    flux = [
        sum(arrived[s, h * 16 : h * 16 + 16, :].astype(F32) for s in range(NLON)) for h in range(2)
    ]
    blocks = jnp.concatenate(
        [flux[f // 2][:, (f % 2) * 128 : (f % 2) * 128 + 128] for f in range(4)], axis=0
    ).astype(BF)
    contribution = jnp.zeros((64, 128), F32)
    for m in range(16):
        product = dot(blocks, regrid[m], ((1,), (1,)))
        contribution = jnp.where(offset[...] == m, product, contribution)
    contribution = contribution.astype(BF)
    out_row = lax.broadcasted_iota(jnp.int32, (16, 64), 0)
    in_row = lax.broadcasted_iota(jnp.int32, (16, 64), 1)
    same_field = lax.rem(out_row, 4) == in_row // 16
    same_row = out_row // 4 == lax.rem(in_row, 16) // 4
    is_wet = out_row // 4 < wet[0, 0]
    gather = jnp.where(
        jnp.logical_and(jnp.logical_and(same_field, same_row), is_wet), 1.0, 0.0
    ).astype(BF)
    cells = dot(gather, contribution, ((1,), (0,)))
    cells_high, cells_low = split_two(cells)
    cells_pair = jnp.concatenate([cells_high, cells_low], axis=0)
    pair_row = lax.broadcasted_iota(jnp.int32, (32, CH), 0)
    field_weights = jnp.concatenate([flux_weight[...].astype(F32)] * 8, axis=0)
    flux_part = jnp.zeros((32, CH), F32)
    for r in range(ROWS):
        lo, hi = r * CELLS, (r + 1) * CELLS
        mine = lax.rem(pair_row, 16) // 4 == r
        weights = jnp.where(mine, field_weights, 0.0).astype(BF)
        act_grad = dot(cot[lo:hi, :], mix[...], ((1,), (1,)))
        act_grad = act_grad + dot(cells_pair, weights, ((0,), (0,)))
        value = hidden[lo:hi, :]
        gate = jax.nn.sigmoid(value)
        activation = (value * gate).astype(BF)
        grad = (act_grad * gate * (1.0 + value * (1.0 - gate))).astype(BF)
        hg_out[lo:hi, :] = grad
        turned[3, :, lo:hi] = activation.T
        flux_part = flux_part + jnp.where(
            mine, dot(cells_pair, activation, ((1,), (0,))), 0.0
        )
    scale = 1.0 / 512.0
    flux_total = jnp.zeros((4, CH), F32)
    for part in range(8):
        flux_total = flux_total + flux_part[part * 4 : part * 4 + 4]
    flux_high, flux_low = split_two(flux_total * scale)
    flux_rows = jnp.concatenate([flux_high.astype(F32), flux_low.astype(F32)], axis=0)
    for q in range(3):
        turned[q] = shifted[q].T
    for t in range(9):
        start = (t // 3) * CELLS
        product = dot(turned[t % 3, :, start : start + 512], hg_out[...], ((1,), (0,)))
        grads[t * CH : (t + 1) * CH, :] = product * scale
    product = dot(turned[3, :, 0:512], cot[...], ((1,), (0,)))
    grads[9 * CH : 10 * CH, :] = product * scale
    for m in range(16):
        mine = pl.multiple_of(m * 160 + core * 80, 8)
        other = pl.multiple_of(m * 160 + 80 - core * 80, 8)
        keep_out[m * 80 : m * 80 + 80, :] = grads[pl.ds(mine, 80), :]
        send_out[m * 80 : m * 80 + 80, :] = grads[pl.ds(other, 80), :].astype(BF)
    keep_out[1280:1288, :] = flux_rows
    send_out[1280:1296, :] = jnp.concatenate(
        [flux_rows, jnp.zeros((8, CH), F32)], axis=0
    ).astype(BF)
    first, last = hg_out[0:CELLS, :], hg_out[3 * CELLS : 4 * CELLS, :]
    send_out[1296:1424, :] = jnp.where(core == 0, last, first)
    zrow_out[...] = jnp.where(core == 0, first, last)


def merge_kernel(keep, got, hg, out, total, moved):
    ox = lax.axis_index("ox")
    core = lax.axis_index("core")
    total[...] = keep[0:1280, :] + got[0:1280, :].astype(F32)
    for c in range(NLON):
        for z in range(8):
            for yh in range(2):
                m = yh * 8 + z
                to = c * 320 + (z * 2 + yh) * SHARE
                moved[to : to + SHARE, :] = total[m * 80 + c * SHARE : m * 80 + c * SHARE + SHARE, :]
    flux = keep[1280:1288, :] + got[1280:1296, :].astype(F32)[0:8]
    flux_high, flux_low = split_two(flux[0:4] + flux[4:8])
    inside = got[1296:1424, :]
    pieces = [inside] + own_rows(hg) + [inside, None, None]
    part = lax.broadcasted_iota(jnp.int32, (8, CH), 0)
    drop = jnp.where(core == 0, 0, ROWS + 1)
    first = jnp.where(part == drop, 0.0, edge_cells(pieces, 0))
    last = jnp.where(part == drop, 0.0, edge_cells(pieces, 1))
    for c in range(NLON):
        to_right = jnp.where(lax.rem(ox + 1, NLON) == c, 1.0, 0.0)
        to_left = jnp.where(lax.rem(ox + NLON - 1, NLON) == c, 1.0, 0.0)
        halo = last * to_right + first * to_left
        out[c, 0:320, :] = moved[c * 320 : c * 320 + 320, :].astype(BF)
        out[c, 320:336, :] = jnp.concatenate(
            [flux_high.astype(F32), flux_low.astype(F32), halo], axis=0
        ).astype(BF)


def side_cells(arrived):
    ox = lax.axis_index("ox")
    left = arrived[lax.rem(ox + NLON - 1, NLON), 320:336, :].astype(F32)[8:16]
    right = arrived[lax.rem(ox + 1, NLON), 320:336, :].astype(F32)[8:16]
    return left, right


def corner_kernel(arrived, out):
    core = lax.axis_index("core")
    left, right = side_cells(arrived)
    pair = jnp.where(
        core == 0,
        jnp.concatenate([left[1:2], right[1:2]], axis=0),
        jnp.concatenate([left[4:5], right[4:5]], axis=0),
    )
    out[...] = jnp.concatenate([pair, jnp.zeros((14, CH), F32)], axis=0).astype(BF)


def sum_flux(pieces):
    total = pieces[0]
    for piece in pieces[1:]:
        total = total + piece
    return total[0:4] + total[4:8]


def ox_sum_kernel(got, out):
    for z in range(8):
        piece = got[0, z * 40 : z * 40 + 40, :].astype(F32)
        for s in range(1, NLON):
            piece = piece + got[s, z * 40 : z * 40 + 40, :].astype(F32)
        out[z, 0:40, :] = piece.astype(BF)
    flux = sum_flux([got[s, 320:336, :].astype(F32)[0:8] for s in range(NLON)])
    high, low = split_two(flux)
    rows = jnp.concatenate([high.astype(F32), low.astype(F32)], axis=0).astype(BF)
    for z in range(8):
        out[z, 40:48, :] = rows


def z_sum_kernel(got, out):
    piece = got[0].astype(F32)
    for s in range(1, 8):
        piece = piece + got[s].astype(F32)
    high, low = split_two(piece[40:44] + piece[44:48])
    flux = jnp.concatenate([high.astype(F32), low.astype(F32)], axis=0)
    pad = jnp.zeros((4, CH), F32)
    for yh in range(2):
        rows = jnp.concatenate([piece[yh * SHARE : yh * SHARE + SHARE], pad, flux], axis=0).astype(BF)
        for e in range(4):
            out[e * 2 + yh] = rows


def last_sum_kernel(got, weight_out, flux_out):
    piece = got[0].astype(F32)
    for s in range(1, 8):
        piece = piece + got[s].astype(F32)
    weight_out[...] = piece[0:SHARE]
    flux_out[...] = piece[24:28] + piece[28:32]


def input_kernel(hg, got, across, arrived, corners, cot, conv, out, shifted):
    oy = oy_index()
    core = lax.axis_index("core")
    left, right = side_cells(arrived)
    exists = jnp.where(jnp.logical_or(oy == 0, oy == 31), 0.0, 1.0)
    corner = corners[...].astype(F32) * exists
    part = lax.broadcasted_iota(jnp.int32, (8, CH), 0)
    at = jnp.where(core == 0, 0, ROWS + 1)
    left = jnp.where(part == at, corner[0:1], left)
    right = jnp.where(part == at, corner[1:2], right)
    inside = got[1296:1424, :].astype(F32)
    other = across[...].astype(F32) * exists
    top = jnp.where(core == 0, other, inside)
    bottom = jnp.where(core == 0, inside, other)
    build_shifts(shifted, [top] + own_rows(hg) + [bottom], left, right)
    for half in range(2):
        acc = cot[half * 256 : half * 256 + 256, :].astype(F32)
        for t in range(9):
            start = (2 - t // 3) * CELLS + half * 256
            acc = acc + dot(shifted[2 - t % 3, start : start + 256, :], conv[t], ((1,), (1,)))
        out[half * 256 : half * 256 + 256, :] = acc.astype(BF)


def body(
    state,
    state_cot,
    flux_cot,
    conv_weight,
    mix_weight,
    flux_weight,
    regrid_weights,
    intersection_atm,
    intersection_offset,
    wet_rows,
):
    state = state.reshape(ROWS * CELLS, CH)
    cot = state_cot.reshape(ROWS * CELLS, CH)
    iatm = intersection_atm.reshape(-1)
    ioff = intersection_offset.reshape(-1)
    up, down, state = call(
        first_kernel,
        (
            struct((4 * CELLS, 128), BF),
            struct((CELLS, CH), BF),
            struct((ROWS * CELLS, CH), BF),
        ),
        scratch=[
            pltpu.VMEM((64, 4, 128), BF),
            pltpu.VMEM((256, 128), F32),
            pltpu.SemaphoreType.DMA((2,)),
        ],
        specs=[HBM] * 2,
    )(state, flux_cot.reshape(64, 4, 128))
    below = lax.ppermute(up, OY, [((i + 1) % 32, i) for i in range(32)])
    above = lax.ppermute(down, OY, [(i, (i + 1) % 32) for i in range(32)])
    needed = (cot, conv_weight, mix_weight, flux_weight, regrid_weights)
    pick, offset, cot, conv_weight, mix_weight, flux_weight, regrid_weights = call(
        pick_kernel,
        (struct((64, 128), BF), struct((64, 128), jnp.int32))
        + tuple(struct(a.shape, a.dtype) for a in needed),
        scratch=[pltpu.SemaphoreType.DMA((5,))],
        specs=[SM, SM] + [HBM] * 5,
    )(iatm, ioff, *needed)
    packed = call(pack_kernel, struct((NLON, 48, CH), BF), n_in=5)(pick, state, below, above, up)
    arrived = lax.all_to_all(packed, "ox", 0, 0, tiled=True)
    hg, send, keep, zrow = call(
        main_kernel,
        (
            struct((ROWS * CELLS, CH), BF),
            struct((1424, CH), BF),
            struct((1288, CH), F32),
            struct((CELLS, CH), BF),
        ),
        scratch=[
            pltpu.VMEM((3, 768, CH), BF),
            pltpu.VMEM((4, CH, 768), BF),
            pltpu.VMEM((512, CH), F32),
            pltpu.VMEM((2560, CH), F32),
        ],
        specs=[SM] + [VM] * 10,
    )(wet_rows, offset, state, below, above, arrived, cot, conv_weight, mix_weight, flux_weight, regrid_weights)
    swap = [(i, (i - 1) % 32 if i % 2 == 0 else (i + 1) % 32) for i in range(32)]
    got = lax.ppermute(send, "core", [(0, 1), (1, 0)])
    across = lax.ppermute(zrow, OY, swap)
    packed = call(
        merge_kernel,
        struct((NLON, 336, CH), BF),
        scratch=[pltpu.VMEM((1280, CH), F32), pltpu.VMEM((1280, CH), F32)],
        n_in=3,
    )(keep, got, hg)
    by_ox = lax.all_to_all(packed, "ox", 0, 0, tiled=True)
    corners = call(corner_kernel, struct((16, CH), BF), n_in=1)(by_ox)
    corners = lax.ppermute(corners, OY, swap)
    packed = call(ox_sum_kernel, struct((8, 48, CH), BF), n_in=1)(by_ox)
    by_z = lax.all_to_all(packed, "z", 0, 0, tiled=True)
    packed = call(z_sum_kernel, struct((8, 32, CH), BF), n_in=1)(by_z)
    by_rest = lax.all_to_all(packed, ("ens", "yh"), 0, 0, tiled=True)
    weight_out, flux_out = call(
        last_sum_kernel, (jax.ShapeDtypeStruct((SHARE, CH), F32), jax.ShapeDtypeStruct((4, CH), F32)), n_in=1
    )(by_rest)
    input_grad = call(
        input_kernel,
        jax.ShapeDtypeStruct((ROWS * CELLS, CH), BF),
        scratch=[pltpu.VMEM((3, 768, CH), BF)],
        n_in=7,
    )(hg, got, across, by_ox, corners, cot, conv_weight)
    return (input_grad.reshape(1, ROWS, CELLS, CH), weight_out, flux_out)


def solution(mesh):
    fine = Mesh(mesh.devices.reshape(4, 2, 8, 2, 4), ("ens", "yh", "z", "core", "ox"))
    in_specs = (
        P("ens", OY, "ox", None),
        P("ens", OY, "ox", None),
        P("ens", OY + ("ox",), None, None),
        P(),
        P(),
        P(),
        P(),
        P(),
        P(),
        P(OY, "ox"),
    )
    out_specs = (P("ens", OY, "ox", None), P(OY + ("ox",), None), P())
    return jax.shard_map(body, mesh=fine, in_specs=in_specs, out_specs=out_specs, check_vma=False)
```

```python
import jax
import jax.numpy as jnp
from jax import lax
from jax.experimental import pallas as pl
from jax.experimental.pallas import tpu as pltpu
from jax.sharding import Mesh, PartitionSpec as P


BF = jnp.bfloat16
F32 = jnp.float32
OY = ("yh", "z", "core")
SWAP = [(i, (i - 1) % 32 if i % 2 == 0 else (i + 1) % 32) for i in range(32)]
ROWS = 4
CELLS = 128
CH = 256
NLON = 4
SHARE = 20
VM = pl.BlockSpec(memory_space=pltpu.VMEM)
HBM = pl.BlockSpec(memory_space=pltpu.HBM)
SM = pl.BlockSpec(memory_space=pltpu.SMEM)


def oy_index():
    return lax.axis_index("yh") * 16 + lax.axis_index("z") * 2 + lax.axis_index("core")


def call(kernel, outs, scratch=(), specs=None, n_in=None):
    specs = specs if specs is not None else [VM] * n_in
    run = pl.pallas_call(
        kernel,
        out_shape=outs,
        in_specs=specs,
        out_specs=jax.tree.map(lambda _: VM, outs),
        scratch_shapes=list(scratch),
        compiler_params=pltpu.CompilerParams(vmem_limit_bytes=24 << 20),
    )

    def placed(*args):
        return run(
            *[
                pltpu.with_memory_space_constraint(a, s.memory_space) if s is not SM else a
                for a, s in zip(args, specs)
            ]
        )

    return placed


def struct(shape, dtype):
    return pltpu.VMEM(shape, dtype)


def split_two(value):
    high = value.astype(BF)
    low = (value - high.astype(F32)).astype(BF)
    return high, low


def dot(a, b, dims):
    return lax.dot_general(a, b, (dims, ((), ())), preferred_element_type=F32)


def edge_cells(pieces, edge):
    at, base = (0, 0) if edge == 0 else (15, CELLS - 16)
    rows = []
    for piece in pieces:
        if piece is None:
            rows.append(jnp.zeros((1, CH), F32))
        else:
            rows.append(piece[base : base + 16, :].astype(F32)[at : at + 1])
    return jnp.concatenate(rows, axis=0)


def own_rows(ref):
    return [ref[r * CELLS : (r + 1) * CELLS, :] for r in range(ROWS)]


def joined(ref):
    return jnp.concatenate([ref[0:CELLS, :], ref[CELLS : 2 * CELLS, :]], axis=1)


def halo_rows(outer, inner):
    oy = oy_index()
    core = lax.axis_index("core")
    exists = jnp.where(jnp.logical_or(oy == 0, oy == 31), 0.0, 1.0)
    across, inside = joined(outer).astype(F32) * exists, joined(inner).astype(F32)
    top = jnp.where(core == 0, across, inside)
    bottom = jnp.where(core == 0, inside, across)
    return top.astype(BF), bottom.astype(BF)


def first_kernel(state_in, flux_in, up, down, state, flux, planes, sems):
    copies = [
        pltpu.make_async_copy(state_in, state, sems.at[0]),
        pltpu.make_async_copy(flux_in, flux, sems.at[1]),
    ]
    for copy in copies:
        copy.start()
    for copy in copies:
        copy.wait()
    core = lax.axis_index("core")
    first, last = state[0:CELLS, :], state[3 * CELLS : 4 * CELLS, :]
    outer = jnp.where(core == 0, first, last)
    inner = jnp.where(core == 0, last, first)
    for pay, rows in ((up, outer), (down, inner)):
        pay[0:CELLS, :] = rows[:, 0:128]
        pay[CELLS : 2 * CELLS, :] = rows[:, 128:256]
    for b in range(64):
        block = flux[b].astype(F32)
        for f in range(4):
            planes[f * 64 + b : f * 64 + b + 1, :] = block[f : f + 1]
    packed = planes[...].astype(BF)
    up[2 * CELLS : 4 * CELLS, :] = packed
    down[2 * CELLS : 4 * CELLS, :] = packed


def pick_kernel(iatm, ioff, wet, *refs):
    sources, pick, offset_out, gather_out = refs[:5], refs[5], refs[6], refs[7]
    targets, sems = refs[8:13], refs[13]
    copies = [
        pltpu.make_async_copy(source, target, sems.at[n])
        for n, (source, target) in enumerate(zip(sources, targets))
    ]
    for copy in copies:
        copy.start()
    oy = oy_index()
    ox = lax.axis_index("ox")
    me = (oy * NLON + ox) * 64
    nxt = (lax.rem(oy + 1, 32) * NLON + ox) * 64
    row = lax.broadcasted_iota(jnp.int32, (64, 128), 0)
    lane = lax.broadcasted_iota(jnp.int32, (64, 128), 1)
    target = jnp.zeros((64, 128), jnp.int32)
    offset = jnp.zeros((64, 128), jnp.int32)
    for r in range(ROWS):
        for k in range(4):
            for d in range(NLON):
                value = iatm[d, k, oy * ROWS + r]
                target = jnp.where(row == d * 16 + r * 4 + k, value, target)
            value = ioff[ox, k, oy * ROWS + r]
            offset = jnp.where(lax.rem(row, 16) == r * 4 + k, value, offset)
    wanted = jnp.where(lane < 64, lane + me, lane - 64 + nxt)
    pick[...] = jnp.where(target == wanted, 1.0, 0.0).astype(BF)
    offset_out[...] = offset
    out_row = lax.broadcasted_iota(jnp.int32, (16, 64), 0)
    in_row = lax.broadcasted_iota(jnp.int32, (16, 64), 1)
    same_field = lax.rem(out_row, 4) == in_row // 16
    same_row = out_row // 4 == lax.rem(in_row, 16) // 4
    is_wet = out_row // 4 < wet[0, 0]
    gather_out[...] = jnp.where(
        jnp.logical_and(jnp.logical_and(same_field, same_row), is_wet), 1.0, 0.0
    ).astype(BF)
    for copy in copies:
        copy.wait()


def pack_kernel(pick, state, outer, inner, up, out):
    ox = lax.axis_index("ox")
    core = lax.axis_index("core")
    for f in range(4):
        lo = 2 * CELLS + f * 64
        following = jnp.where(core == 0, inner[lo : lo + 64, :], outer[lo : lo + 64, :])
        source = jnp.concatenate([up[lo : lo + 64, :], following], axis=0)
        got = dot(pick[...], source, ((1,), (0,))).astype(BF)
        for d in range(NLON):
            to = (f % 2) * 128
            out[d, (f // 2) * 16 : (f // 2) * 16 + 16, to : to + 128] = got[d * 16 : d * 16 + 16]
    top, bottom = halo_rows(outer, inner)
    pieces = [top] + own_rows(state) + [bottom]
    first = edge_cells(pieces, 0)
    last = edge_cells(pieces, 1)
    for d in range(NLON):
        to_right = jnp.where(lax.rem(ox + 1, NLON) == d, 1.0, 0.0)
        to_left = jnp.where(lax.rem(ox + NLON - 1, NLON) == d, 1.0, 0.0)
        halo = last * to_right + first * to_left
        out[d, 32:48, :] = jnp.concatenate([halo, jnp.zeros((10, CH), F32)], axis=0).astype(BF)


def build_shifts(shifted, pieces, left, right):
    cell = lax.broadcasted_iota(jnp.int32, (CELLS, CH), 0)
    for r, piece in enumerate(pieces):
        value = piece.astype(F32)
        shifted[1, r * CELLS : (r + 1) * CELLS, :] = piece.astype(BF)
        plus = jnp.where(cell == CELLS - 1, right[r : r + 1, :], pltpu.roll(value, CELLS - 1, 0))
        minus = jnp.where(cell == 0, left[r : r + 1, :], pltpu.roll(value, 1, 0))
        shifted[2, r * CELLS : (r + 1) * CELLS, :] = plus.astype(BF)
        shifted[0, r * CELLS : (r + 1) * CELLS, :] = minus.astype(BF)


def main_kernel(
    gather,
    offset,
    state,
    outer,
    inner,
    arrived,
    cot,
    conv,
    mix,
    flux_weight,
    regrid,
    hg_out,
    send_out,
    keep_out,
    shifted,
    turned,
    hidden,
    grads,
):
    ox = lax.axis_index("ox")
    core = lax.axis_index("core")
    left = arrived[lax.rem(ox + NLON - 1, NLON), 32:48, :].astype(F32)
    right = arrived[lax.rem(ox + 1, NLON), 32:48, :].astype(F32)
    top, bottom = halo_rows(outer, inner)
    build_shifts(shifted, [top] + own_rows(state) + [bottom], left, right)
    for half in range(2):
        acc = jnp.zeros((256, CH), F32)
        for t in range(9):
            start = (t // 3) * CELLS + half * 256
            acc = acc + dot(shifted[t % 3, start : start + 256, :], conv[t], ((1,), (0,)))
        hidden[half * 256 : half * 256 + 256, :] = acc
    flux = [
        sum(arrived[s, h * 16 : h * 16 + 16, :].astype(F32) for s in range(NLON)) for h in range(2)
    ]
    blocks = jnp.concatenate(
        [flux[f // 2][:, (f % 2) * 128 : (f % 2) * 128 + 128] for f in range(4)], axis=0
    ).astype(BF)
    contribution = jnp.zeros((64, 128), F32)
    for m in range(16):
        product = dot(blocks, regrid[m], ((1,), (1,)))
        contribution = jnp.where(offset[...] == m, product, contribution)
    contribution = contribution.astype(BF)
    cells = dot(gather[...], contribution, ((1,), (0,)))
    cells_high, cells_low = split_two(cells)
    cells_pair = jnp.concatenate([cells_high, cells_low], axis=0)
    pair_row = lax.broadcasted_iota(jnp.int32, (32, CH), 0)
    field_weights = jnp.concatenate([flux_weight[...].astype(F32)] * 8, axis=0)
    flux_part = jnp.zeros((32, CH), F32)
    for r in range(ROWS):
        lo, hi = r * CELLS, (r + 1) * CELLS
        mine = lax.rem(pair_row, 16) // 4 == r
        weights = jnp.where(mine, field_weights, 0.0).astype(BF)
        act_grad = dot(cot[lo:hi, :], mix[...], ((1,), (1,)))
        act_grad = act_grad + dot(cells_pair, weights, ((0,), (0,)))
        value = hidden[lo:hi, :]
        gate = jax.nn.sigmoid(value)
        activation = (value * gate).astype(BF)
        grad = (act_grad * gate * (1.0 + value * (1.0 - gate))).astype(BF)
        hg_out[lo:hi, :] = grad
        turned[3, :, lo:hi] = activation.T
        flux_part = flux_part + jnp.where(
            mine, dot(cells_pair, activation, ((1,), (0,))), 0.0
        )
    scale = 1.0 / 512.0
    flux_total = jnp.zeros((4, CH), F32)
    for part in range(8):
        flux_total = flux_total + flux_part[part * 4 : part * 4 + 4]
    flux_high, flux_low = split_two(flux_total * scale)
    flux_rows = jnp.concatenate([flux_high.astype(F32), flux_low.astype(F32)], axis=0)
    for q in range(3):
        turned[q] = shifted[q].T
    for t in range(9):
        start = (t // 3) * CELLS
        product = dot(turned[t % 3, :, start : start + 512], hg_out[...], ((1,), (0,)))
        grads[t * CH : (t + 1) * CH, :] = product * scale
    product = dot(turned[3, :, 0:512], cot[...], ((1,), (0,)))
    grads[9 * CH : 10 * CH, :] = product * scale
    for m in range(16):
        mine = pl.multiple_of(m * 160 + core * 80, 8)
        other = pl.multiple_of(m * 160 + 80 - core * 80, 8)
        keep_out[m * 80 : m * 80 + 80, :] = grads[pl.ds(mine, 80), :]
        send_out[m * 80 : m * 80 + 80, :] = grads[pl.ds(other, 80), :].astype(BF)
    keep_out[1280:1288, :] = flux_rows
    send_out[1280:1296, :] = jnp.concatenate(
        [flux_rows, jnp.zeros((8, CH), F32)], axis=0
    ).astype(BF)
    first, last = hg_out[0:CELLS, :], hg_out[3 * CELLS : 4 * CELLS, :]
    send_out[1296:1424, :] = jnp.where(core == 0, last, first)


def row_kernel(hg, out):
    core = lax.axis_index("core")
    out[...] = jnp.where(core == 0, hg[0:CELLS, :], hg[3 * CELLS : 4 * CELLS, :])


def merge_kernel(keep, got, hg, out, total, moved):
    ox = lax.axis_index("ox")
    core = lax.axis_index("core")
    total[...] = keep[0:1280, :] + got[0:1280, :].astype(F32)
    for c in range(NLON):
        for z in range(8):
            for yh in range(2):
                m = yh * 8 + z
                to = c * 320 + (z * 2 + yh) * SHARE
                moved[to : to + SHARE, :] = total[m * 80 + c * SHARE : m * 80 + c * SHARE + SHARE, :]
    flux = keep[1280:1288, :] + got[1280:1296, :].astype(F32)[0:8]
    flux_high, flux_low = split_two(flux[0:4] + flux[4:8])
    inside = got[1296:1424, :]
    pieces = [inside] + own_rows(hg) + [inside, None, None]
    part = lax.broadcasted_iota(jnp.int32, (8, CH), 0)
    drop = jnp.where(core == 0, 0, ROWS + 1)
    first = jnp.where(part == drop, 0.0, edge_cells(pieces, 0))
    last = jnp.where(part == drop, 0.0, edge_cells(pieces, 1))
    for c in range(NLON):
        to_right = jnp.where(lax.rem(ox + 1, NLON) == c, 1.0, 0.0)
        to_left = jnp.where(lax.rem(ox + NLON - 1, NLON) == c, 1.0, 0.0)
        halo = last * to_right + first * to_left
        out[c, 0:320, :] = moved[c * 320 : c * 320 + 320, :].astype(BF)
        out[c, 320:336, :] = jnp.concatenate(
            [flux_high.astype(F32), flux_low.astype(F32), halo], axis=0
        ).astype(BF)


def side_cells(arrived):
    ox = lax.axis_index("ox")
    left = arrived[lax.rem(ox + NLON - 1, NLON), 320:336, :].astype(F32)[8:16]
    right = arrived[lax.rem(ox + 1, NLON), 320:336, :].astype(F32)[8:16]
    return left, right


def corner_kernel(arrived, out):
    core = lax.axis_index("core")
    left, right = side_cells(arrived)
    pair = jnp.where(
        core == 0,
        jnp.concatenate([left[1:2], right[1:2]], axis=0),
        jnp.concatenate([left[4:5], right[4:5]], axis=0),
    )
    out[...] = jnp.concatenate([pair, jnp.zeros((14, CH), F32)], axis=0).astype(BF)


def sum_flux(pieces):
    total = pieces[0]
    for piece in pieces[1:]:
        total = total + piece
    return total[0:4] + total[4:8]


def ox_sum_kernel(got, out):
    for z in range(8):
        piece = got[0, z * 40 : z * 40 + 40, :].astype(F32)
        for s in range(1, NLON):
            piece = piece + got[s, z * 40 : z * 40 + 40, :].astype(F32)
        out[z, 0:40, :] = piece.astype(BF)
    flux = sum_flux([got[s, 320:336, :].astype(F32)[0:8] for s in range(NLON)])
    high, low = split_two(flux)
    rows = jnp.concatenate([high.astype(F32), low.astype(F32)], axis=0).astype(BF)
    for z in range(8):
        out[z, 40:48, :] = rows


def z_sum_kernel(got, out):
    piece = got[0].astype(F32)
    for s in range(1, 8):
        piece = piece + got[s].astype(F32)
    high, low = split_two(piece[40:44] + piece[44:48])
    flux = jnp.concatenate([high.astype(F32), low.astype(F32)], axis=0)
    pad = jnp.zeros((4, CH), F32)
    for yh in range(2):
        rows = jnp.concatenate([piece[yh * SHARE : yh * SHARE + SHARE], pad, flux], axis=0).astype(BF)
        for e in range(4):
            out[e * 2 + yh] = rows


def last_sum_kernel(got, weight_out, flux_out):
    piece = got[0].astype(F32)
    for s in range(1, 8):
        piece = piece + got[s].astype(F32)
    weight_out[...] = piece[0:SHARE]
    flux_out[...] = piece[24:28] + piece[28:32]


def spread_kernel(hg, got, across, cot, conv, out, shifted):
    oy = oy_index()
    core = lax.axis_index("core")
    exists = jnp.where(jnp.logical_or(oy == 0, oy == 31), 0.0, 1.0)
    inside = got[1296:1424, :].astype(F32)
    other = across[...].astype(F32) * exists
    top = jnp.where(core == 0, other, inside)
    bottom = jnp.where(core == 0, inside, other)
    nothing = jnp.zeros((8, CH), F32)
    build_shifts(shifted, [top] + own_rows(hg) + [bottom], nothing, nothing)
    for half in range(2):
        acc = cot[half * 256 : half * 256 + 256, :].astype(F32)
        for t in range(9):
            start = (2 - t // 3) * CELLS + half * 256
            acc = acc + dot(shifted[2 - t % 3, start : start + 256, :], conv[t], ((1,), (1,)))
        out[half * 256 : half * 256 + 256, :] = acc


def input_kernel(partial, arrived, corners, conv, out):
    oy = oy_index()
    core = lax.axis_index("core")
    exists = jnp.where(jnp.logical_or(oy == 0, oy == 31), 0.0, 1.0)
    corner = corners[...].astype(F32) * exists
    part = lax.broadcasted_iota(jnp.int32, (8, CH), 0)
    at = jnp.where(core == 0, 0, ROWS + 1)
    out[...] = partial[...].astype(BF)
    slab = lax.broadcasted_iota(jnp.int32, (16, CH), 0)
    for side, cells in enumerate(side_cells(arrived)):
        cells = jnp.where(part == at, corner[side : side + 1], cells)
        cells = jnp.concatenate([cells, jnp.zeros((8, CH), F32)], axis=0).astype(BF)
        added = jnp.zeros((ROWS, CH), F32)
        for p in (-1, 0, 1):
            product = dot(cells, conv[3 * (p + 1) + 2 - 2 * side], ((1,), (1,)))
            added = added + product[1 - p : 1 - p + ROWS]
        for r in range(ROWS):
            to = r * CELLS + side * (CELLS - 16)
            value = partial[to : to + 16, :]
            value = jnp.where(slab == side * 15, value + added[r : r + 1], value)
            out[to : to + 16, :] = value.astype(BF)


def body(
    state,
    state_cot,
    flux_cot,
    conv_weight,
    mix_weight,
    flux_weight,
    regrid_weights,
    intersection_atm,
    intersection_offset,
    wet_rows,
):
    state = state.reshape(ROWS * CELLS, CH)
    cot = state_cot.reshape(ROWS * CELLS, CH)
    up, down, state = call(
        first_kernel,
        (
            struct((4 * CELLS, 128), BF),
            struct((4 * CELLS, 128), BF),
            struct((ROWS * CELLS, CH), BF),
        ),
        scratch=[
            pltpu.VMEM((64, 4, 128), BF),
            pltpu.VMEM((256, 128), F32),
            pltpu.SemaphoreType.DMA((2,)),
        ],
        specs=[HBM] * 2,
    )(state, flux_cot.reshape(64, 4, 128))
    outer = lax.ppermute(up, OY, SWAP)
    inner = lax.ppermute(down, "core", [(0, 1), (1, 0)])
    needed = (cot, conv_weight, mix_weight, flux_weight, regrid_weights)
    pick, offset, gather, cot, conv_weight, mix_weight, flux_weight, regrid_weights = call(
        pick_kernel,
        (struct((64, 128), BF), struct((64, 128), jnp.int32), struct((16, 64), BF))
        + tuple(struct(a.shape, a.dtype) for a in needed),
        scratch=[pltpu.SemaphoreType.DMA((5,))],
        specs=[SM] * 3 + [HBM] * 5,
    )(
        intersection_atm.transpose(1, 2, 0),
        intersection_offset.transpose(1, 2, 0),
        wet_rows,
        *needed,
    )
    packed = call(pack_kernel, struct((NLON, 48, CH), BF), n_in=5)(pick, state, outer, inner, up)
    arrived = lax.all_to_all(packed, "ox", 0, 0, tiled=True)
    hg, send, keep = call(
        main_kernel,
        (
            struct((ROWS * CELLS, CH), BF),
            struct((1424, CH), BF),
            struct((1288, CH), F32),
        ),
        scratch=[
            pltpu.VMEM((3, 768, CH), BF),
            pltpu.VMEM((4, CH, 768), BF),
            pltpu.VMEM((512, CH), F32),
            pltpu.VMEM((2560, CH), F32),
        ],
        n_in=11,
    )(gather, offset, state, outer, inner, arrived, cot, conv_weight, mix_weight, flux_weight, regrid_weights)
    got = lax.ppermute(send, "core", [(0, 1), (1, 0)])
    zrow = call(row_kernel, struct((CELLS, CH), BF), n_in=1)(hg)
    across = lax.ppermute(zrow, OY, SWAP)
    packed = call(
        merge_kernel,
        struct((NLON, 336, CH), BF),
        scratch=[pltpu.VMEM((1280, CH), F32), pltpu.VMEM((1280, CH), F32)],
        n_in=3,
    )(keep, got, hg)
    by_ox = lax.all_to_all(packed, "ox", 0, 0, tiled=True)
    corners = call(corner_kernel, struct((16, CH), BF), n_in=1)(by_ox)
    corners = lax.ppermute(corners, OY, SWAP)
    packed = call(ox_sum_kernel, struct((8, 48, CH), BF), n_in=1)(by_ox)
    by_z = lax.all_to_all(packed, "z", 0, 0, tiled=True)
    packed = call(z_sum_kernel, struct((8, 32, CH), BF), n_in=1)(by_z)
    by_rest = lax.all_to_all(packed, ("ens", "yh"), 0, 0, tiled=True)
    weight_out, flux_out = call(
        last_sum_kernel, (jax.ShapeDtypeStruct((SHARE, CH), F32), jax.ShapeDtypeStruct((4, CH), F32)), n_in=1
    )(by_rest)
    partial = call(
        spread_kernel,
        struct((ROWS * CELLS, CH), F32),
        scratch=[pltpu.VMEM((3, 768, CH), BF)],
        n_in=5,
    )(hg, got, across, cot, conv_weight)
    input_grad = call(input_kernel, jax.ShapeDtypeStruct((ROWS * CELLS, CH), BF), n_in=4)(
        partial, by_ox, corners, conv_weight
    )
    return (input_grad.reshape(1, ROWS, CELLS, CH), weight_out, flux_out)


def solution(mesh):
    fine = Mesh(mesh.devices.reshape(4, 2, 8, 2, 4), ("ens", "yh", "z", "core", "ox"))
    in_specs = (
        P("ens", OY, "ox", None),
        P("ens", OY, "ox", None),
        P("ens", OY + ("ox",), None, None),
        P(),
        P(),
        P(),
        P(),
        P(),
        P(),
        P(OY, "ox"),
    )
    out_specs = (P("ens", OY, "ox", None), P(OY + ("ox",), None), P())

    return jax.shard_map(body, mesh=fine, in_specs=in_specs, out_specs=out_specs, check_vma=False)
```

```python
import jax
import jax.numpy as jnp
from jax import lax
from jax.experimental import pallas as pl
from jax.experimental.pallas import tpu as pltpu
from jax.sharding import Mesh, PartitionSpec as P


BF = jnp.bfloat16
F32 = jnp.float32
OY = ("yh", "z", "core")
SWAP = [(i, (i - 1) % 32 if i % 2 == 0 else (i + 1) % 32) for i in range(32)]
ROWS = 4
CELLS = 128
CH = 256
NLON = 4
SHARE = 20
VM = pl.BlockSpec(memory_space=pltpu.VMEM)
HBM = pl.BlockSpec(memory_space=pltpu.HBM)
ANY = pl.BlockSpec(memory_space=pl.ANY)
SM = pl.BlockSpec(memory_space=pltpu.SMEM)


def oy_index():
    return lax.axis_index("yh") * 16 + lax.axis_index("z") * 2 + lax.axis_index("core")


def call(kernel, outs, scratch=(), specs=None, n_in=None):
    specs = specs if specs is not None else [VM] * n_in
    run = pl.pallas_call(
        kernel,
        out_shape=outs,
        in_specs=specs,
        out_specs=jax.tree.map(lambda _: VM, outs),
        scratch_shapes=list(scratch),
        compiler_params=pltpu.CompilerParams(vmem_limit_bytes=24 << 20),
    )

    def placed(*args):
        return run(
            *[
                pltpu.with_memory_space_constraint(a, s.memory_space) if s not in (SM, ANY) else a
                for a, s in zip(args, specs)
            ]
        )

    return placed


def struct(shape, dtype):
    return pltpu.VMEM(shape, dtype)


def split_two(value):
    high = value.astype(BF)
    low = (value - high.astype(F32)).astype(BF)
    return high, low


def dot(a, b, dims):
    return lax.dot_general(a, b, (dims, ((), ())), preferred_element_type=F32)


def edge_cells(pieces, edge):
    at, base = (0, 0) if edge == 0 else (15, CELLS - 16)
    rows = []
    for piece in pieces:
        if piece is None:
            rows.append(jnp.zeros((1, CH), F32))
        else:
            rows.append(piece[base : base + 16, :].astype(F32)[at : at + 1])
    return jnp.concatenate(rows, axis=0)


def own_rows(ref):
    return [ref[r * CELLS : (r + 1) * CELLS, :] for r in range(ROWS)]


def joined(ref):
    return jnp.concatenate([ref[0:CELLS, :], ref[CELLS : 2 * CELLS, :]], axis=1)


def halo_rows(outer, inner):
    oy = oy_index()
    core = lax.axis_index("core")
    exists = jnp.where(jnp.logical_or(oy == 0, oy == 31), 0.0, 1.0)
    across, inside = joined(outer).astype(F32) * exists, joined(inner).astype(F32)
    top = jnp.where(core == 0, across, inside)
    bottom = jnp.where(core == 0, inside, across)
    return top.astype(BF), bottom.astype(BF)


def first_kernel(state_in, flux_in, up, down, state, flux, planes, sems):
    copies = [
        pltpu.make_async_copy(state_in, state, sems.at[0]),
        pltpu.make_async_copy(flux_in, flux, sems.at[1]),
    ]
    for copy in copies:
        copy.start()
    for copy in copies:
        copy.wait()
    core = lax.axis_index("core")
    first, last = state[0:CELLS, :], state[3 * CELLS : 4 * CELLS, :]
    outer = jnp.where(core == 0, first, last)
    inner = jnp.where(core == 0, last, first)
    for pay, rows in ((up, outer), (down, inner)):
        pay[0:CELLS, :] = rows[:, 0:128]
        pay[CELLS : 2 * CELLS, :] = rows[:, 128:256]
    for b in range(64):
        block = flux[b].astype(F32)
        for f in range(4):
            planes[f * 64 + b : f * 64 + b + 1, :] = block[f : f + 1]
    packed = planes[...].astype(BF)
    up[2 * CELLS : 4 * CELLS, :] = packed
    down[2 * CELLS : 4 * CELLS, :] = packed


def pick_kernel(*refs):
    sources, pick, offset_out, gather_out = refs[:8], refs[8], refs[9], refs[10]
    sources, wet = sources[:2] + sources[3:], sources[2]
    iatm, ioff, sems = refs[16:19]
    targets = (iatm, ioff) + refs[11:16]
    copies = [
        pltpu.make_async_copy(source, target, sems.at[n])
        for n, (source, target) in enumerate(zip(sources, targets))
    ]
    for copy in copies:
        copy.start()
    for copy in copies[:2]:
        copy.wait()
    oy = oy_index()
    ox = lax.axis_index("ox")
    me = (oy * NLON + ox) * 64
    nxt = (lax.rem(oy + 1, 32) * NLON + ox) * 64
    row = lax.broadcasted_iota(jnp.int32, (64, 128), 0)
    lane = lax.broadcasted_iota(jnp.int32, (64, 128), 1)
    target = jnp.zeros((64, 128), jnp.int32)
    offset = jnp.zeros((64, 128), jnp.int32)
    for r in range(ROWS):
        for k in range(4):
            for d in range(NLON):
                value = iatm[d, k, oy * ROWS + r]
                target = jnp.where(row == d * 16 + r * 4 + k, value, target)
            value = ioff[ox, k, oy * ROWS + r]
            offset = jnp.where(lax.rem(row, 16) == r * 4 + k, value, offset)
    wanted = jnp.where(lane < 64, lane + me, lane - 64 + nxt)
    pick[...] = jnp.where(target == wanted, 1.0, 0.0).astype(BF)
    offset_out[...] = offset
    out_row = lax.broadcasted_iota(jnp.int32, (16, 64), 0)
    in_row = lax.broadcasted_iota(jnp.int32, (16, 64), 1)
    same_field = lax.rem(out_row, 4) == in_row // 16
    same_row = out_row // 4 == lax.rem(in_row, 16) // 4
    is_wet = out_row // 4 < wet[0, 0]
    gather_out[...] = jnp.where(
        jnp.logical_and(jnp.logical_and(same_field, same_row), is_wet), 1.0, 0.0
    ).astype(BF)
    for copy in copies[2:]:
        copy.wait()


def pack_kernel(pick, state, outer, inner, up, out):
    ox = lax.axis_index("ox")
    core = lax.axis_index("core")
    for f in range(4):
        lo = 2 * CELLS + f * 64
        following = jnp.where(core == 0, inner[lo : lo + 64, :], outer[lo : lo + 64, :])
        source = jnp.concatenate([up[lo : lo + 64, :], following], axis=0)
        got = dot(pick[...], source, ((1,), (0,))).astype(BF)
        for d in range(NLON):
            to = (f % 2) * 128
            out[d, (f // 2) * 16 : (f // 2) * 16 + 16, to : to + 128] = got[d * 16 : d * 16 + 16]
    top, bottom = halo_rows(outer, inner)
    pieces = [top] + own_rows(state) + [bottom]
    first = edge_cells(pieces, 0)
    last = edge_cells(pieces, 1)
    for d in range(NLON):
        to_right = jnp.where(lax.rem(ox + 1, NLON) == d, 1.0, 0.0)
        to_left = jnp.where(lax.rem(ox + NLON - 1, NLON) == d, 1.0, 0.0)
        halo = last * to_right + first * to_left
        out[d, 32:48, :] = jnp.concatenate([halo, jnp.zeros((10, CH), F32)], axis=0).astype(BF)


def build_shifts(shifted, pieces, left, right):
    cell = lax.broadcasted_iota(jnp.int32, (CELLS, CH), 0)
    for r, piece in enumerate(pieces):
        value = piece.astype(F32)
        shifted[1, r * CELLS : (r + 1) * CELLS, :] = piece.astype(BF)
        plus = jnp.where(cell == CELLS - 1, right[r : r + 1, :], pltpu.roll(value, CELLS - 1, 0))
        minus = jnp.where(cell == 0, left[r : r + 1, :], pltpu.roll(value, 1, 0))
        shifted[2, r * CELLS : (r + 1) * CELLS, :] = plus.astype(BF)
        shifted[0, r * CELLS : (r + 1) * CELLS, :] = minus.astype(BF)


def main_kernel(
    gather,
    offset,
    state,
    outer,
    inner,
    arrived,
    cot,
    conv,
    mix,
    flux_weight,
    regrid,
    hg_out,
    send_out,
    keep_out,
    shifted,
    turned,
    hidden,
    grads,
):
    ox = lax.axis_index("ox")
    core = lax.axis_index("core")
    left = arrived[lax.rem(ox + NLON - 1, NLON), 32:48, :].astype(F32)
    right = arrived[lax.rem(ox + 1, NLON), 32:48, :].astype(F32)
    top, bottom = halo_rows(outer, inner)
    build_shifts(shifted, [top] + own_rows(state) + [bottom], left, right)
    for half in range(2):
        acc = jnp.zeros((256, CH), F32)
        for t in range(9):
            start = (t // 3) * CELLS + half * 256
            acc = acc + dot(shifted[t % 3, start : start + 256, :], conv[t], ((1,), (0,)))
        hidden[half * 256 : half * 256 + 256, :] = acc
    flux = [
        sum(arrived[s, h * 16 : h * 16 + 16, :].astype(F32) for s in range(NLON)) for h in range(2)
    ]
    blocks = jnp.concatenate(
        [flux[f // 2][:, (f % 2) * 128 : (f % 2) * 128 + 128] for f in range(4)], axis=0
    ).astype(BF)
    contribution = jnp.zeros((64, 128), F32)
    for m in range(16):
        product = dot(blocks, regrid[m], ((1,), (1,)))
        contribution = jnp.where(offset[...] == m, product, contribution)
    contribution = contribution.astype(BF)
    cells = dot(gather[...], contribution, ((1,), (0,)))
    cells_high, cells_low = split_two(cells)
    cells_pair = jnp.concatenate([cells_high, cells_low], axis=0)
    pair_row = lax.broadcasted_iota(jnp.int32, (32, CH), 0)
    field_weights = jnp.concatenate([flux_weight[...].astype(F32)] * 8, axis=0)
    flux_part = jnp.zeros((32, CH), F32)
    for r in range(ROWS):
        lo, hi = r * CELLS, (r + 1) * CELLS
        mine = lax.rem(pair_row, 16) // 4 == r
        weights = jnp.where(mine, field_weights, 0.0).astype(BF)
        act_grad = dot(cot[lo:hi, :], mix[...], ((1,), (1,)))
        act_grad = act_grad + dot(cells_pair, weights, ((0,), (0,)))
        value = hidden[lo:hi, :]
        gate = jax.nn.sigmoid(value)
        activation = (value * gate).astype(BF)
        grad = (act_grad * gate * (1.0 + value * (1.0 - gate))).astype(BF)
        hg_out[lo:hi, :] = grad
        turned[3, :, lo:hi] = activation.T
        flux_part = flux_part + jnp.where(
            mine, dot(cells_pair, activation, ((1,), (0,))), 0.0
        )
    scale = 1.0 / 512.0
    flux_total = jnp.zeros((4, CH), F32)
    for part in range(8):
        flux_total = flux_total + flux_part[part * 4 : part * 4 + 4]
    flux_high, flux_low = split_two(flux_total * scale)
    flux_rows = jnp.concatenate([flux_high.astype(F32), flux_low.astype(F32)], axis=0)
    for q in range(3):
        turned[q] = shifted[q].T
    for t in range(9):
        start = (t // 3) * CELLS
        product = dot(turned[t % 3, :, start : start + 512], hg_out[...], ((1,), (0,)))
        grads[t * CH : (t + 1) * CH, :] = product * scale
    product = dot(turned[3, :, 0:512], cot[...], ((1,), (0,)))
    grads[9 * CH : 10 * CH, :] = product * scale
    for m in range(16):
        mine = pl.multiple_of(m * 160 + core * 80, 8)
        other = pl.multiple_of(m * 160 + 80 - core * 80, 8)
        keep_out[m * 80 : m * 80 + 80, :] = grads[pl.ds(mine, 80), :]
        send_out[m * 80 : m * 80 + 80, :] = grads[pl.ds(other, 80), :].astype(BF)
    keep_out[1280:1288, :] = flux_rows
    send_out[1280:1296, :] = jnp.concatenate(
        [flux_rows, jnp.zeros((8, CH), F32)], axis=0
    ).astype(BF)
    first, last = hg_out[0:CELLS, :], hg_out[3 * CELLS : 4 * CELLS, :]
    send_out[1296:1424, :] = jnp.where(core == 0, last, first)


def row_kernel(hg, out):
    core = lax.axis_index("core")
    out[...] = jnp.where(core == 0, hg[0:CELLS, :], hg[3 * CELLS : 4 * CELLS, :])


def merge_kernel(keep, got, hg, out, padded, total, moved):
    ox = lax.axis_index("ox")
    core = lax.axis_index("core")
    total[...] = keep[0:1280, :] + got[0:1280, :].astype(F32)
    for c in range(NLON):
        for z in range(8):
            for yh in range(2):
                m = yh * 8 + z
                to = c * 320 + (z * 2 + yh) * SHARE
                moved[to : to + SHARE, :] = total[m * 80 + c * SHARE : m * 80 + c * SHARE + SHARE, :]
    flux = keep[1280:1288, :] + got[1280:1296, :].astype(F32)[0:8]
    flux_high, flux_low = split_two(flux[0:4] + flux[4:8])
    inside = got[1296:1424, :]
    padded[0:CELLS, :] = inside
    padded[CELLS : 5 * CELLS, :] = hg[...]
    padded[5 * CELLS : 6 * CELLS, :] = inside
    pieces = [inside] + own_rows(hg) + [inside, None, None]
    part = lax.broadcasted_iota(jnp.int32, (8, CH), 0)
    drop = jnp.where(core == 0, 0, ROWS + 1)
    first = jnp.where(part == drop, 0.0, edge_cells(pieces, 0))
    last = jnp.where(part == drop, 0.0, edge_cells(pieces, 1))
    for c in range(NLON):
        to_right = jnp.where(lax.rem(ox + 1, NLON) == c, 1.0, 0.0)
        to_left = jnp.where(lax.rem(ox + NLON - 1, NLON) == c, 1.0, 0.0)
        halo = last * to_right + first * to_left
        out[c, 0:320, :] = moved[c * 320 : c * 320 + 320, :].astype(BF)
        out[c, 320:336, :] = jnp.concatenate(
            [flux_high.astype(F32), flux_low.astype(F32), halo], axis=0
        ).astype(BF)


def side_cells(arrived):
    ox = lax.axis_index("ox")
    left = arrived[lax.rem(ox + NLON - 1, NLON), 320:336, :].astype(F32)[8:16]
    right = arrived[lax.rem(ox + 1, NLON), 320:336, :].astype(F32)[8:16]
    return left, right


def corner_kernel(arrived, out):
    core = lax.axis_index("core")
    left, right = side_cells(arrived)
    pair = jnp.where(
        core == 0,
        jnp.concatenate([left[1:2], right[1:2]], axis=0),
        jnp.concatenate([left[4:5], right[4:5]], axis=0),
    )
    out[...] = jnp.concatenate([pair, jnp.zeros((14, CH), F32)], axis=0).astype(BF)


def sum_flux(pieces):
    total = pieces[0]
    for piece in pieces[1:]:
        total = total + piece
    return total[0:4] + total[4:8]


def ox_sum_kernel(got, out):
    for z in range(8):
        piece = got[0, z * 40 : z * 40 + 40, :].astype(F32)
        for s in range(1, NLON):
            piece = piece + got[s, z * 40 : z * 40 + 40, :].astype(F32)
        out[z, 0:40, :] = piece.astype(BF)
    flux = sum_flux([got[s, 320:336, :].astype(F32)[0:8] for s in range(NLON)])
    high, low = split_two(flux)
    rows = jnp.concatenate([high.astype(F32), low.astype(F32)], axis=0).astype(BF)
    for z in range(8):
        out[z, 40:48, :] = rows


def z_sum_kernel(got, out):
    piece = got[0].astype(F32)
    for s in range(1, 8):
        piece = piece + got[s].astype(F32)
    high, low = split_two(piece[40:44] + piece[44:48])
    flux = jnp.concatenate([high.astype(F32), low.astype(F32)], axis=0)
    pad = jnp.zeros((4, CH), F32)
    for yh in range(2):
        rows = jnp.concatenate([piece[yh * SHARE : yh * SHARE + SHARE], pad, flux], axis=0).astype(BF)
        for e in range(4):
            out[e * 2 + yh] = rows


def last_sum_kernel(got, weight_out, flux_out):
    piece = got[0].astype(F32)
    for s in range(1, 8):
        piece = piece + got[s].astype(F32)
    weight_out[...] = piece[0:SHARE]
    flux_out[...] = piece[24:28] + piece[28:32]


def spread_kernel(padded, across, cot, conv, out, shifted):
    oy = oy_index()
    core = lax.axis_index("core")
    exists = jnp.where(jnp.logical_or(oy == 0, oy == 31), 0.0, 1.0)
    inside = padded[0:CELLS, :].astype(F32)
    other = across[...].astype(F32) * exists
    top = jnp.where(core == 0, other, inside)
    bottom = jnp.where(core == 0, inside, other)
    nothing = jnp.zeros((8, CH), F32)
    own = [padded[r * CELLS : (r + 1) * CELLS, :] for r in range(1, ROWS + 1)]
    build_shifts(shifted, [top] + own + [bottom], nothing, nothing)
    for half in range(2):
        acc = cot[half * 256 : half * 256 + 256, :].astype(F32)
        for t in range(9):
            start = (2 - t // 3) * CELLS + half * 256
            acc = acc + dot(shifted[2 - t % 3, start : start + 256, :], conv[t], ((1,), (1,)))
        out[half * 256 : half * 256 + 256, :] = acc


def input_kernel(partial, arrived, corners, conv, out):
    oy = oy_index()
    core = lax.axis_index("core")
    exists = jnp.where(jnp.logical_or(oy == 0, oy == 31), 0.0, 1.0)
    corner = corners[...].astype(F32) * exists
    part = lax.broadcasted_iota(jnp.int32, (8, CH), 0)
    at = jnp.where(core == 0, 0, ROWS + 1)
    out[...] = partial[...].astype(BF)
    slab = lax.broadcasted_iota(jnp.int32, (16, CH), 0)
    for side, cells in enumerate(side_cells(arrived)):
        cells = jnp.where(part == at, corner[side : side + 1], cells)
        cells = jnp.concatenate([cells, jnp.zeros((8, CH), F32)], axis=0).astype(BF)
        added = jnp.zeros((ROWS, CH), F32)
        for p in (-1, 0, 1):
            product = dot(cells, conv[3 * (p + 1) + 2 - 2 * side], ((1,), (1,)))
            added = added + product[1 - p : 1 - p + ROWS]
        for r in range(ROWS):
            to = r * CELLS + side * (CELLS - 16)
            value = partial[to : to + 16, :]
            value = jnp.where(slab == side * 15, value + added[r : r + 1], value)
            out[to : to + 16, :] = value.astype(BF)


def body(
    state,
    state_cot,
    flux_cot,
    conv_weight,
    mix_weight,
    flux_weight,
    regrid_weights,
    intersection_atm,
    intersection_offset,
    wet_rows,
):
    state = state.reshape(ROWS * CELLS, CH)
    cot = state_cot.reshape(ROWS * CELLS, CH)
    up, down, state = call(
        first_kernel,
        (
            struct((4 * CELLS, 128), BF),
            struct((4 * CELLS, 128), BF),
            struct((ROWS * CELLS, CH), BF),
        ),
        scratch=[
            pltpu.VMEM((64, 4, 128), BF),
            pltpu.VMEM((256, 128), F32),
            pltpu.SemaphoreType.DMA((2,)),
        ],
        specs=[HBM] * 2,
    )(state, flux_cot.reshape(64, 4, 128))
    outer = lax.ppermute(up, OY, SWAP)
    inner = lax.ppermute(down, "core", [(0, 1), (1, 0)])
    needed = (cot, conv_weight, mix_weight, flux_weight, regrid_weights)
    pick, offset, gather, cot, conv_weight, mix_weight, flux_weight, regrid_weights = call(
        pick_kernel,
        (struct((64, 128), BF), struct((64, 128), jnp.int32), struct((16, 64), BF))
        + tuple(struct(a.shape, a.dtype) for a in needed),
        scratch=[
            pltpu.SMEM((4, 4, 128), jnp.int32),
            pltpu.SMEM((4, 4, 128), jnp.int32),
            pltpu.SemaphoreType.DMA((7,)),
        ],
        specs=[HBM] * 2 + [SM] + [HBM] * 5,
    )(
        intersection_atm.transpose(1, 2, 0),
        intersection_offset.transpose(1, 2, 0),
        wet_rows,
        *needed,
    )
    packed = call(pack_kernel, struct((NLON, 48, CH), BF), n_in=5)(pick, state, outer, inner, up)
    arrived = lax.all_to_all(packed, "ox", 0, 0, tiled=True)
    hg, send, keep = call(
        main_kernel,
        (
            struct((ROWS * CELLS, CH), BF),
            struct((1424, CH), BF),
            struct((1288, CH), F32),
        ),
        scratch=[
            pltpu.VMEM((3, 768, CH), BF),
            pltpu.VMEM((4, CH, 768), BF),
            pltpu.VMEM((512, CH), F32),
            pltpu.VMEM((2560, CH), F32),
        ],
        n_in=11,
    )(gather, offset, state, outer, inner, arrived, cot, conv_weight, mix_weight, flux_weight, regrid_weights)
    got = lax.ppermute(send, "core", [(0, 1), (1, 0)])
    zrow = call(row_kernel, struct((CELLS, CH), BF), n_in=1)(hg)
    across = lax.ppermute(zrow, OY, SWAP)
    packed, padded = call(
        merge_kernel,
        (struct((NLON, 336, CH), BF), struct((768, CH), BF)),
        scratch=[pltpu.VMEM((1280, CH), F32), pltpu.VMEM((1280, CH), F32)],
        n_in=3,
    )(keep, got, hg)
    by_ox = lax.all_to_all(packed, "ox", 0, 0, tiled=True)
    corners = call(corner_kernel, struct((16, CH), BF), n_in=1)(by_ox)
    corners = lax.ppermute(corners, OY, SWAP)
    packed = call(ox_sum_kernel, struct((8, 48, CH), BF), n_in=1)(by_ox)
    by_z = lax.all_to_all(packed, "z", 0, 0, tiled=True)
    packed = call(z_sum_kernel, struct((8, 32, CH), BF), n_in=1)(by_z)
    by_rest = lax.all_to_all(packed, ("ens", "yh"), 0, 0, tiled=True)
    weight_out, flux_out = call(
        last_sum_kernel, (jax.ShapeDtypeStruct((SHARE, CH), F32), jax.ShapeDtypeStruct((4, CH), F32)), n_in=1
    )(by_rest)
    partial = call(
        spread_kernel,
        struct((ROWS * CELLS, CH), F32),
        scratch=[pltpu.VMEM((3, 768, CH), BF)],
        n_in=4,
    )(padded, across, cot, conv_weight)
    input_grad = call(input_kernel, jax.ShapeDtypeStruct((ROWS * CELLS, CH), BF), n_in=4)(
        partial, by_ox, corners, conv_weight
    )
    return (input_grad.reshape(1, ROWS, CELLS, CH), weight_out, flux_out)


def solution(mesh):
    fine = Mesh(mesh.devices.reshape(4, 2, 8, 2, 4), ("ens", "yh", "z", "core", "ox"))
    in_specs = (
        P("ens", OY, "ox", None),
        P("ens", OY, "ox", None),
        P("ens", OY + ("ox",), None, None),
        P(),
        P(),
        P(),
        P(),
        P(),
        P(),
        P(OY, "ox"),
    )
    out_specs = (P("ens", OY, "ox", None), P(OY + ("ox",), None), P())

    return jax.shard_map(body, mesh=fine, in_specs=in_specs, out_specs=out_specs, check_vma=False)
```

```python
import jax
import jax.numpy as jnp
from jax import lax
from jax.experimental import pallas as pl
from jax.experimental.pallas import tpu as pltpu
from jax.sharding import Mesh, PartitionSpec as P


BF = jnp.bfloat16
F32 = jnp.float32
OY = ("yh", "z", "core")
SWAP = [(i, (i - 1) % 32 if i % 2 == 0 else (i + 1) % 32) for i in range(32)]
ROWS = 4
CELLS = 128
CH = 256
NLON = 4
SHARE = 20
SCALE = 1.0 / 512.0
VM = pl.BlockSpec(memory_space=pltpu.VMEM)
HBM = pl.BlockSpec(memory_space=pltpu.HBM)
ANY = pl.BlockSpec(memory_space=pl.ANY)
SM = pl.BlockSpec(memory_space=pltpu.SMEM)


def oy_index():
    return lax.axis_index("yh") * 16 + lax.axis_index("z") * 2 + lax.axis_index("core")


def call(kernel, outs, scratch=(), specs=None, n_in=None):
    specs = specs if specs is not None else [VM] * n_in
    run = pl.pallas_call(
        kernel,
        out_shape=outs,
        in_specs=specs,
        out_specs=jax.tree.map(lambda _: VM, outs),
        scratch_shapes=list(scratch),
        compiler_params=pltpu.CompilerParams(vmem_limit_bytes=24 << 20),
    )

    def placed(*args):
        return run(
            *[
                pltpu.with_memory_space_constraint(a, s.memory_space) if s not in (SM, ANY) else a
                for a, s in zip(args, specs)
            ]
        )

    return placed


def struct(shape, dtype):
    return pltpu.VMEM(shape, dtype)


def split_two(value):
    high = value.astype(BF)
    low = (value - high.astype(F32)).astype(BF)
    return high, low


def dot(a, b, dims):
    return lax.dot_general(a, b, (dims, ((), ())), preferred_element_type=F32)


def edge_cells(pieces, edge):
    at, base = (0, 0) if edge == 0 else (15, CELLS - 16)
    rows = []
    for piece in pieces:
        if piece is None:
            rows.append(jnp.zeros((1, CH), F32))
        else:
            rows.append(piece[base : base + 16, :].astype(F32)[at : at + 1])
    return jnp.concatenate(rows, axis=0)


def own_rows(ref):
    return [ref[r * CELLS : (r + 1) * CELLS, :] for r in range(ROWS)]


def joined(ref):
    return jnp.concatenate([ref[0:CELLS, :], ref[CELLS : 2 * CELLS, :]], axis=1)


def halo_rows(outer, inner):
    oy = oy_index()
    core = lax.axis_index("core")
    exists = jnp.where(jnp.logical_or(oy == 0, oy == 31), 0.0, 1.0)
    across, inside = joined(outer).astype(F32) * exists, joined(inner).astype(F32)
    top = jnp.where(core == 0, across, inside)
    bottom = jnp.where(core == 0, inside, across)
    return top.astype(BF), bottom.astype(BF)


def first_kernel(state_in, flux_in, up, down, state, flux, planes, sems):
    copies = [
        pltpu.make_async_copy(state_in, state, sems.at[0]),
        pltpu.make_async_copy(flux_in, flux, sems.at[1]),
    ]
    for copy in copies:
        copy.start()
    for copy in copies:
        copy.wait()
    core = lax.axis_index("core")
    first, last = state[0:CELLS, :], state[3 * CELLS : 4 * CELLS, :]
    outer = jnp.where(core == 0, first, last)
    inner = jnp.where(core == 0, last, first)
    for pay, rows in ((up, outer), (down, inner)):
        pay[0:CELLS, :] = rows[:, 0:128]
        pay[CELLS : 2 * CELLS, :] = rows[:, 128:256]
    for b in range(64):
        block = flux[b].astype(F32)
        for f in range(4):
            planes[f * 64 + b : f * 64 + b + 1, :] = block[f : f + 1]
    packed = planes[...].astype(BF)
    up[2 * CELLS : 4 * CELLS, :] = packed
    down[2 * CELLS : 4 * CELLS, :] = packed


def pick_kernel(*refs):
    sources, pick, offset_out, gather_out = refs[:8], refs[8], refs[9], refs[10]
    sources, wet = sources[:2] + sources[3:], sources[2]
    iatm, ioff, mix, sems = refs[16:20]
    act_base, cot, conv, flux_weight, regrid = refs[11:16]
    targets = (iatm, ioff, cot, conv, mix, flux_weight, regrid)
    copies = [
        pltpu.make_async_copy(source, target, sems.at[n])
        for n, (source, target) in enumerate(zip(sources, targets))
    ]
    for copy in copies:
        copy.start()
    for copy in copies[:2]:
        copy.wait()
    oy = oy_index()
    ox = lax.axis_index("ox")
    me = (oy * NLON + ox) * 64
    nxt = (lax.rem(oy + 1, 32) * NLON + ox) * 64
    row = lax.broadcasted_iota(jnp.int32, (64, 128), 0)
    lane = lax.broadcasted_iota(jnp.int32, (64, 128), 1)
    target = jnp.zeros((64, 128), jnp.int32)
    offset = jnp.zeros((64, 128), jnp.int32)
    for r in range(ROWS):
        for k in range(4):
            for d in range(NLON):
                value = iatm[d, k, oy * ROWS + r]
                target = jnp.where(row == d * 16 + r * 4 + k, value, target)
            value = ioff[ox, k, oy * ROWS + r]
            offset = jnp.where(lax.rem(row, 16) == r * 4 + k, value, offset)
    wanted = jnp.where(lane < 64, lane + me, lane - 64 + nxt)
    pick[...] = jnp.where(target == wanted, 1.0, 0.0).astype(BF)
    offset_out[...] = offset
    out_row = lax.broadcasted_iota(jnp.int32, (16, 64), 0)
    in_row = lax.broadcasted_iota(jnp.int32, (16, 64), 1)
    same_field = lax.rem(out_row, 4) == in_row // 16
    same_row = out_row // 4 == lax.rem(in_row, 16) // 4
    is_wet = out_row // 4 < wet[0, 0]
    gather_out[...] = jnp.where(
        jnp.logical_and(jnp.logical_and(same_field, same_row), is_wet), 1.0, 0.0
    ).astype(BF)
    for copy in copies[2:]:
        copy.wait()
    act_base[...] = dot(cot[...], mix[...], ((1,), (1,)))


def pack_kernel(pick, state, outer, inner, up, out):
    ox = lax.axis_index("ox")
    core = lax.axis_index("core")
    for f in range(4):
        lo = 2 * CELLS + f * 64
        following = jnp.where(core == 0, inner[lo : lo + 64, :], outer[lo : lo + 64, :])
        source = jnp.concatenate([up[lo : lo + 64, :], following], axis=0)
        got = dot(pick[...], source, ((1,), (0,))).astype(BF)
        for d in range(NLON):
            to = (f % 2) * 128
            out[d, (f // 2) * 16 : (f // 2) * 16 + 16, to : to + 128] = got[d * 16 : d * 16 + 16]
    top, bottom = halo_rows(outer, inner)
    pieces = [top] + own_rows(state) + [bottom]
    first = edge_cells(pieces, 0)
    last = edge_cells(pieces, 1)
    for d in range(NLON):
        to_right = jnp.where(lax.rem(ox + 1, NLON) == d, 1.0, 0.0)
        to_left = jnp.where(lax.rem(ox + NLON - 1, NLON) == d, 1.0, 0.0)
        halo = last * to_right + first * to_left
        out[d, 32:48, :] = jnp.concatenate([halo, jnp.zeros((10, CH), F32)], axis=0).astype(BF)


def build_shifts(shifted, pieces, left, right):
    cell = lax.broadcasted_iota(jnp.int32, (CELLS, CH), 0)
    for r, piece in enumerate(pieces):
        value = piece.astype(F32)
        shifted[1, r * CELLS : (r + 1) * CELLS, :] = piece.astype(BF)
        plus = jnp.where(cell == CELLS - 1, right[r : r + 1, :], pltpu.roll(value, CELLS - 1, 0))
        minus = jnp.where(cell == 0, left[r : r + 1, :], pltpu.roll(value, 1, 0))
        shifted[2, r * CELLS : (r + 1) * CELLS, :] = plus.astype(BF)
        shifted[0, r * CELLS : (r + 1) * CELLS, :] = minus.astype(BF)


def main_kernel(
    gather,
    offset,
    state,
    outer,
    inner,
    arrived,
    cot,
    conv,
    act_base,
    flux_weight,
    regrid,
    hg_out,
    send_out,
    grads,
    flux_out,
    shifted,
    turned,
    hidden,
):
    ox = lax.axis_index("ox")
    core = lax.axis_index("core")
    left = arrived[lax.rem(ox + NLON - 1, NLON), 32:48, :].astype(F32)
    right = arrived[lax.rem(ox + 1, NLON), 32:48, :].astype(F32)
    top, bottom = halo_rows(outer, inner)
    build_shifts(shifted, [top] + own_rows(state) + [bottom], left, right)
    for half in range(2):
        acc = jnp.zeros((256, CH), F32)
        for t in range(9):
            start = (t // 3) * CELLS + half * 256
            acc = acc + dot(shifted[t % 3, start : start + 256, :], conv[t], ((1,), (0,)))
        hidden[half * 256 : half * 256 + 256, :] = acc
    flux = [
        sum(arrived[s, h * 16 : h * 16 + 16, :].astype(F32) for s in range(NLON)) for h in range(2)
    ]
    blocks = jnp.concatenate(
        [flux[f // 2][:, (f % 2) * 128 : (f % 2) * 128 + 128] for f in range(4)], axis=0
    ).astype(BF)
    contribution = jnp.zeros((64, 128), F32)
    for m in range(8):
        product = dot(blocks, regrid[m], ((1,), (1,)))
        for side in range(2):
            part = product[:, side * 128 : side * 128 + 128]
            contribution = jnp.where(offset[...] == 2 * m + side, part, contribution)
    contribution = contribution.astype(BF)
    cells = dot(gather[...], contribution, ((1,), (0,)))
    cells_high, cells_low = split_two(cells)
    cells_pair = jnp.concatenate([cells_high, cells_low], axis=0)
    pair_row = lax.broadcasted_iota(jnp.int32, (32, CH), 0)
    field_weights = jnp.concatenate([flux_weight[...].astype(F32)] * 8, axis=0)
    flux_part = jnp.zeros((32, CH), F32)
    for r in range(ROWS):
        lo, hi = r * CELLS, (r + 1) * CELLS
        mine = lax.rem(pair_row, 16) // 4 == r
        weights = jnp.where(mine, field_weights, 0.0).astype(BF)
        act_grad = act_base[lo:hi, :] + dot(cells_pair, weights, ((0,), (0,)))
        value = hidden[lo:hi, :]
        gate = jax.nn.sigmoid(value)
        activation = (value * gate).astype(BF)
        grad = (act_grad * gate * (1.0 + value * (1.0 - gate))).astype(BF)
        hg_out[lo:hi, :] = grad
        turned[3, :, lo:hi] = activation.T
        flux_part = flux_part + jnp.where(
            mine, dot(cells_pair, activation, ((1,), (0,))), 0.0
        )
    flux_total = jnp.zeros((4, CH), F32)
    for part in range(8):
        flux_total = flux_total + flux_part[part * 4 : part * 4 + 4]
    flux_high, flux_low = split_two(flux_total)
    flux_rows = jnp.concatenate([flux_high.astype(F32), flux_low.astype(F32)], axis=0)
    for q in range(3):
        turned[q] = shifted[q].T
    for t in range(9):
        start = (t // 3) * CELLS
        product = dot(turned[t % 3, :, start : start + 512], hg_out[...], ((1,), (0,)))
        grads[t * CH : (t + 1) * CH, :] = product
    product = dot(turned[3, :, 0:512], cot[...], ((1,), (0,)))
    grads[9 * CH : 10 * CH, :] = product
    for m in range(16):
        other = pl.multiple_of(m * 160 + 80 - core * 80, 8)
        send_out[m * 80 : m * 80 + 80, :] = grads[pl.ds(other, 80), :].astype(BF)
    flux_out[...] = flux_rows
    send_out[1280:1296, :] = jnp.concatenate(
        [flux_rows, jnp.zeros((8, CH), F32)], axis=0
    ).astype(BF)
    first, last = hg_out[0:CELLS, :], hg_out[3 * CELLS : 4 * CELLS, :]
    send_out[1296:1424, :] = jnp.where(core == 0, last, first)


def row_kernel(hg, out):
    core = lax.axis_index("core")
    out[...] = jnp.where(core == 0, hg[0:CELLS, :], hg[3 * CELLS : 4 * CELLS, :])


def merge_kernel(grads, flux_rows, got, hg, out, padded, total, moved):
    ox = lax.axis_index("ox")
    core = lax.axis_index("core")
    for m in range(16):
        lo, hi = m * 80, m * 80 + 80
        mine = pl.multiple_of(m * 160 + core * 80, 8)
        total[lo:hi, :] = grads[pl.ds(mine, 80), :] + got[lo:hi, :].astype(F32)
    for c in range(NLON):
        for z in range(8):
            for yh in range(2):
                m = yh * 8 + z
                to = c * 320 + (z * 2 + yh) * SHARE
                moved[to : to + SHARE, :] = total[m * 80 + c * SHARE : m * 80 + c * SHARE + SHARE, :]
    flux = flux_rows[...] + got[1280:1296, :].astype(F32)[0:8]
    flux_high, flux_low = split_two(flux[0:4] + flux[4:8])
    inside = got[1296:1424, :]
    padded[0:CELLS, :] = inside
    padded[CELLS : 5 * CELLS, :] = hg[...]
    padded[5 * CELLS : 6 * CELLS, :] = inside
    pieces = [inside] + own_rows(hg) + [inside, None, None]
    part = lax.broadcasted_iota(jnp.int32, (8, CH), 0)
    drop = jnp.where(core == 0, 0, ROWS + 1)
    first = jnp.where(part == drop, 0.0, edge_cells(pieces, 0))
    last = jnp.where(part == drop, 0.0, edge_cells(pieces, 1))
    for c in range(NLON):
        to_right = jnp.where(lax.rem(ox + 1, NLON) == c, 1.0, 0.0)
        to_left = jnp.where(lax.rem(ox + NLON - 1, NLON) == c, 1.0, 0.0)
        halo = last * to_right + first * to_left
        out[c, 0:320, :] = moved[c * 320 : c * 320 + 320, :].astype(BF)
        out[c, 320:336, :] = jnp.concatenate(
            [flux_high.astype(F32), flux_low.astype(F32), halo], axis=0
        ).astype(BF)


def side_cells(arrived):
    ox = lax.axis_index("ox")
    left = arrived[lax.rem(ox + NLON - 1, NLON), 320:336, :].astype(F32)[8:16]
    right = arrived[lax.rem(ox + 1, NLON), 320:336, :].astype(F32)[8:16]
    return left, right


def corner_kernel(arrived, out):
    core = lax.axis_index("core")
    left, right = side_cells(arrived)
    pair = jnp.where(
        core == 0,
        jnp.concatenate([left[1:2], right[1:2]], axis=0),
        jnp.concatenate([left[4:5], right[4:5]], axis=0),
    )
    out[...] = jnp.concatenate([pair, jnp.zeros((14, CH), F32)], axis=0).astype(BF)


def sum_flux(pieces):
    total = pieces[0]
    for piece in pieces[1:]:
        total = total + piece
    return total[0:4] + total[4:8]


def ox_sum_kernel(got, out):
    for z in range(8):
        piece = got[0, z * 40 : z * 40 + 40, :].astype(F32)
        for s in range(1, NLON):
            piece = piece + got[s, z * 40 : z * 40 + 40, :].astype(F32)
        out[z, 0:40, :] = piece.astype(BF)
    flux = sum_flux([got[s, 320:336, :].astype(F32)[0:8] for s in range(NLON)])
    high, low = split_two(flux)
    rows = jnp.concatenate([high.astype(F32), low.astype(F32)], axis=0).astype(BF)
    for z in range(8):
        out[z, 40:48, :] = rows


def z_sum_kernel(got, out):
    piece = got[0].astype(F32)
    for s in range(1, 8):
        piece = piece + got[s].astype(F32)
    flux = piece[40:44] + piece[44:48]
    for yh in range(2):
        rows = jnp.concatenate([piece[yh * SHARE : yh * SHARE + SHARE], flux], axis=0).astype(BF)
        for e in range(4):
            out[e * 2 + yh] = rows


def last_sum_kernel(got, weight_out, flux_out):
    piece = got[0].astype(F32)
    for s in range(1, 8):
        piece = piece + got[s].astype(F32)
    weight_out[...] = piece[0:SHARE] * SCALE
    flux_out[...] = piece[SHARE : SHARE + 4] * SCALE


def spread_kernel(padded, across, cot, conv, out, shifted):
    oy = oy_index()
    core = lax.axis_index("core")
    exists = jnp.where(jnp.logical_or(oy == 0, oy == 31), 0.0, 1.0)
    inside = padded[0:CELLS, :].astype(F32)
    other = across[...].astype(F32) * exists
    top = jnp.where(core == 0, other, inside)
    bottom = jnp.where(core == 0, inside, other)
    nothing = jnp.zeros((8, CH), F32)
    own = [padded[r * CELLS : (r + 1) * CELLS, :] for r in range(1, ROWS + 1)]
    build_shifts(shifted, [top] + own + [bottom], nothing, nothing)
    for half in range(2):
        acc = cot[half * 256 : half * 256 + 256, :].astype(F32)
        for t in range(9):
            start = (2 - t // 3) * CELLS + half * 256
            acc = acc + dot(shifted[2 - t % 3, start : start + 256, :], conv[t], ((1,), (1,)))
        out[half * 256 : half * 256 + 256, :] = acc


def input_kernel(partial, arrived, corners, conv, out):
    oy = oy_index()
    core = lax.axis_index("core")
    exists = jnp.where(jnp.logical_or(oy == 0, oy == 31), 0.0, 1.0)
    corner = corners[...].astype(F32) * exists
    part = lax.broadcasted_iota(jnp.int32, (8, CH), 0)
    at = jnp.where(core == 0, 0, ROWS + 1)
    out[...] = partial[...].astype(BF)
    slab = lax.broadcasted_iota(jnp.int32, (16, CH), 0)
    for side, cells in enumerate(side_cells(arrived)):
        cells = jnp.where(part == at, corner[side : side + 1], cells)
        cells = jnp.concatenate([cells, jnp.zeros((8, CH), F32)], axis=0).astype(BF)
        added = jnp.zeros((ROWS, CH), F32)
        for p in (-1, 0, 1):
            product = dot(cells, conv[3 * (p + 1) + 2 - 2 * side], ((1,), (1,)))
            added = added + product[1 - p : 1 - p + ROWS]
        for r in range(ROWS):
            to = r * CELLS + side * (CELLS - 16)
            value = partial[to : to + 16, :]
            value = jnp.where(slab == side * 15, value + added[r : r + 1], value)
            out[to : to + 16, :] = value.astype(BF)


def body(
    state,
    state_cot,
    flux_cot,
    conv_weight,
    mix_weight,
    flux_weight,
    regrid_weights,
    intersection_atm,
    intersection_offset,
    wet_rows,
):
    state = state.reshape(ROWS * CELLS, CH)
    cot = state_cot.reshape(ROWS * CELLS, CH)
    up, down, state = call(
        first_kernel,
        (
            struct((4 * CELLS, 128), BF),
            struct((4 * CELLS, 128), BF),
            struct((ROWS * CELLS, CH), BF),
        ),
        scratch=[
            pltpu.VMEM((64, 4, 128), BF),
            pltpu.VMEM((256, 128), F32),
            pltpu.SemaphoreType.DMA((2,)),
        ],
        specs=[HBM] * 2,
    )(state, flux_cot.reshape(64, 4, 128))
    outer = lax.ppermute(up, OY, SWAP)
    inner = lax.ppermute(down, "core", [(0, 1), (1, 0)])
    regrid_weights = regrid_weights.reshape(8, 256, 128)
    needed = (cot, conv_weight, mix_weight, flux_weight, regrid_weights)
    pick, offset, gather, act_base, cot, conv_weight, flux_weight, regrid_weights = call(
        pick_kernel,
        (struct((64, 128), BF), struct((64, 128), jnp.int32), struct((16, 64), BF))
        + (struct((ROWS * CELLS, CH), F32),)
        + tuple(struct(a.shape, a.dtype) for a in needed if a is not mix_weight),
        scratch=[
            pltpu.SMEM((4, 4, 128), jnp.int32),
            pltpu.SMEM((4, 4, 128), jnp.int32),
            pltpu.VMEM((CH, CH), BF),
            pltpu.SemaphoreType.DMA((7,)),
        ],
        specs=[HBM] * 2 + [SM] + [HBM] * 5,
    )(
        intersection_atm.transpose(1, 2, 0),
        intersection_offset.transpose(1, 2, 0),
        wet_rows,
        *needed,
    )
    packed = call(pack_kernel, struct((NLON, 48, CH), BF), n_in=5)(pick, state, outer, inner, up)
    arrived = lax.all_to_all(packed, "ox", 0, 0, tiled=True)
    hg, send, grads, flux_rows = call(
        main_kernel,
        (
            struct((ROWS * CELLS, CH), BF),
            struct((1424, CH), BF),
            struct((2560, CH), F32),
            struct((8, CH), F32),
        ),
        scratch=[
            pltpu.VMEM((3, 768, CH), BF),
            pltpu.VMEM((4, CH, 768), BF),
            pltpu.VMEM((512, CH), F32),
        ],
        n_in=11,
    )(gather, offset, state, outer, inner, arrived, cot, conv_weight, act_base, flux_weight, regrid_weights)
    got = lax.ppermute(send, "core", [(0, 1), (1, 0)])
    zrow = call(row_kernel, struct((CELLS, CH), BF), n_in=1)(hg)
    across = lax.ppermute(zrow, OY, SWAP)
    packed, padded = call(
        merge_kernel,
        (struct((NLON, 336, CH), BF), struct((768, CH), BF)),
        scratch=[pltpu.VMEM((1280, CH), F32), pltpu.VMEM((1280, CH), F32)],
        n_in=4,
    )(grads, flux_rows, got, hg)
    by_ox = lax.all_to_all(packed, "ox", 0, 0, tiled=True)
    corners = call(corner_kernel, struct((16, CH), BF), n_in=1)(by_ox)
    corners = lax.ppermute(corners, OY, SWAP)
    packed = call(ox_sum_kernel, struct((8, 48, CH), BF), n_in=1)(by_ox)
    by_z = lax.all_to_all(packed, "z", 0, 0, tiled=True)
    packed = call(z_sum_kernel, struct((8, 24, CH), BF), n_in=1)(by_z)
    by_rest = lax.all_to_all(packed, ("ens", "yh"), 0, 0, tiled=True)
    weight_out, flux_out = call(
        last_sum_kernel, (jax.ShapeDtypeStruct((SHARE, CH), F32), jax.ShapeDtypeStruct((4, CH), F32)), n_in=1
    )(by_rest)
    partial = call(
        spread_kernel,
        struct((ROWS * CELLS, CH), F32),
        scratch=[pltpu.VMEM((3, 768, CH), BF)],
        n_in=4,
    )(padded, across, cot, conv_weight)
    input_grad = call(input_kernel, jax.ShapeDtypeStruct((ROWS * CELLS, CH), BF), n_in=4)(
        partial, by_ox, corners, conv_weight
    )
    return (input_grad.reshape(1, ROWS, CELLS, CH), weight_out, flux_out)


def solution(mesh):
    fine = Mesh(mesh.devices.reshape(4, 2, 8, 2, 4), ("ens", "yh", "z", "core", "ox"))
    in_specs = (
        P("ens", OY, "ox", None),
        P("ens", OY, "ox", None),
        P("ens", OY + ("ox",), None, None),
        P(),
        P(),
        P(),
        P(),
        P(),
        P(),
        P(OY, "ox"),
    )
    out_specs = (P("ens", OY, "ox", None), P(OY + ("ox",), None), P())

    return jax.shard_map(body, mesh=fine, in_specs=in_specs, out_specs=out_specs, check_vma=False)
```

```python
import jax
import jax.numpy as jnp
from jax import lax
from jax.experimental import pallas as pl
from jax.experimental.pallas import tpu as pltpu
from jax.sharding import Mesh, PartitionSpec as P


BF = jnp.bfloat16
F32 = jnp.float32
OY = ("yh", "z", "core")
SWAP = [(i, (i - 1) % 32 if i % 2 == 0 else (i + 1) % 32) for i in range(32)]
ROWS = 4
CELLS = 128
CH = 256
NLON = 4
SHARE = 20
SCALE = 1.0 / 512.0
VM = pl.BlockSpec(memory_space=pltpu.VMEM)
HBM = pl.BlockSpec(memory_space=pltpu.HBM)
ANY = pl.BlockSpec(memory_space=pl.ANY)
SM = pl.BlockSpec(memory_space=pltpu.SMEM)


def oy_index():
    return lax.axis_index("yh") * 16 + lax.axis_index("z") * 2 + lax.axis_index("core")


def call(kernel, outs, scratch=(), specs=None, n_in=None, outs_at=None, aliases={}):
    specs = specs if specs is not None else [VM] * n_in
    run = pl.pallas_call(
        kernel,
        out_shape=outs,
        in_specs=specs,
        out_specs=outs_at if outs_at is not None else jax.tree.map(lambda _: VM, outs),
        input_output_aliases=aliases,
        scratch_shapes=list(scratch),
        compiler_params=pltpu.CompilerParams(vmem_limit_bytes=24 << 20),
    )

    def placed(*args):
        return run(
            *[
                pltpu.with_memory_space_constraint(a, s.memory_space) if s not in (SM, ANY) else a
                for a, s in zip(args, specs)
            ]
        )

    return placed


def struct(shape, dtype):
    return pltpu.VMEM(shape, dtype)


def split_two(value):
    high = value.astype(BF)
    low = (value - high.astype(F32)).astype(BF)
    return high, low


def dot(a, b, dims):
    return lax.dot_general(a, b, (dims, ((), ())), preferred_element_type=F32)


def edge_cells(pieces, edge):
    at, base = (0, 0) if edge == 0 else (15, CELLS - 16)
    rows = []
    for piece in pieces:
        if piece is None:
            rows.append(jnp.zeros((1, CH), F32))
        else:
            rows.append(piece[base : base + 16, :].astype(F32)[at : at + 1])
    return jnp.concatenate(rows, axis=0)


def own_rows(ref):
    return [ref[r * CELLS : (r + 1) * CELLS, :] for r in range(ROWS)]


def joined(ref):
    return jnp.concatenate([ref[0:CELLS, :], ref[CELLS : 2 * CELLS, :]], axis=1)


def halo_rows(outer, inner):
    oy = oy_index()
    core = lax.axis_index("core")
    exists = jnp.where(jnp.logical_or(oy == 0, oy == 31), 0.0, 1.0)
    across, inside = joined(outer).astype(F32) * exists, joined(inner).astype(F32)
    top = jnp.where(core == 0, across, inside)
    bottom = jnp.where(core == 0, inside, across)
    return top.astype(BF), bottom.astype(BF)


def first_kernel(state_in, flux_in, up, down, state, flux, planes, sems):
    copies = [
        pltpu.make_async_copy(state_in, state, sems.at[0]),
        pltpu.make_async_copy(flux_in, flux, sems.at[1]),
    ]
    for copy in copies:
        copy.start()
    for copy in copies:
        copy.wait()
    core = lax.axis_index("core")
    first, last = state[0:CELLS, :], state[3 * CELLS : 4 * CELLS, :]
    outer = jnp.where(core == 0, first, last)
    inner = jnp.where(core == 0, last, first)
    for pay, rows in ((up, outer), (down, inner)):
        pay[0:CELLS, :] = rows[:, 0:128]
        pay[CELLS : 2 * CELLS, :] = rows[:, 128:256]
    for b in range(64):
        block = flux[b].astype(F32)
        for f in range(4):
            planes[f * 64 + b : f * 64 + b + 1, :] = block[f : f + 1]
    packed = planes[...].astype(BF)
    up[2 * CELLS : 4 * CELLS, :] = packed
    down[2 * CELLS : 4 * CELLS, :] = packed


def pick_kernel(*refs):
    sources, pick, offset_out, gather_out = refs[:8], refs[8], refs[9], refs[10]
    sources, wet = sources[:2] + sources[3:], sources[2]
    iatm, ioff, mix, sems = refs[16:20]
    act_base, cot, conv, flux_weight, regrid = refs[11:16]
    targets = (iatm, ioff, cot, conv, mix, flux_weight, regrid)
    copies = [
        pltpu.make_async_copy(source, target, sems.at[n])
        for n, (source, target) in enumerate(zip(sources, targets))
    ]
    for copy in copies:
        copy.start()
    for copy in copies[:2]:
        copy.wait()
    oy = oy_index()
    ox = lax.axis_index("ox")
    me = (oy * NLON + ox) * 64
    nxt = (lax.rem(oy + 1, 32) * NLON + ox) * 64
    row = lax.broadcasted_iota(jnp.int32, (64, 128), 0)
    lane = lax.broadcasted_iota(jnp.int32, (64, 128), 1)
    target = jnp.zeros((64, 128), jnp.int32)
    offset = jnp.zeros((64, 128), jnp.int32)
    for r in range(ROWS):
        for k in range(4):
            for d in range(NLON):
                value = iatm[d, k, oy * ROWS + r]
                target = jnp.where(row == d * 16 + r * 4 + k, value, target)
            value = ioff[ox, k, oy * ROWS + r]
            offset = jnp.where(lax.rem(row, 16) == r * 4 + k, value, offset)
    wanted = jnp.where(lane < 64, lane + me, lane - 64 + nxt)
    pick[...] = jnp.where(target == wanted, 1.0, 0.0).astype(BF)
    offset_out[...] = offset
    out_row = lax.broadcasted_iota(jnp.int32, (16, 64), 0)
    in_row = lax.broadcasted_iota(jnp.int32, (16, 64), 1)
    same_field = lax.rem(out_row, 4) == in_row // 16
    same_row = out_row // 4 == lax.rem(in_row, 16) // 4
    is_wet = out_row // 4 < wet[0, 0]
    gather_out[...] = jnp.where(
        jnp.logical_and(jnp.logical_and(same_field, same_row), is_wet), 1.0, 0.0
    ).astype(BF)
    for copy in copies[2:]:
        copy.wait()
    act_base[...] = dot(cot[...], mix[...], ((1,), (1,)))


def pack_kernel(pick, state, outer, inner, up, out):
    ox = lax.axis_index("ox")
    core = lax.axis_index("core")
    for f in range(4):
        lo = 2 * CELLS + f * 64
        following = jnp.where(core == 0, inner[lo : lo + 64, :], outer[lo : lo + 64, :])
        source = jnp.concatenate([up[lo : lo + 64, :], following], axis=0)
        got = dot(pick[...], source, ((1,), (0,))).astype(BF)
        for d in range(NLON):
            to = (f % 2) * 128
            out[d, (f // 2) * 16 : (f // 2) * 16 + 16, to : to + 128] = got[d * 16 : d * 16 + 16]
    top, bottom = halo_rows(outer, inner)
    pieces = [top] + own_rows(state) + [bottom]
    first = edge_cells(pieces, 0)
    last = edge_cells(pieces, 1)
    for d in range(NLON):
        to_right = jnp.where(lax.rem(ox + 1, NLON) == d, 1.0, 0.0)
        to_left = jnp.where(lax.rem(ox + NLON - 1, NLON) == d, 1.0, 0.0)
        halo = last * to_right + first * to_left
        out[d, 32:48, :] = jnp.concatenate([halo, jnp.zeros((10, CH), F32)], axis=0).astype(BF)


def build_shifts(shifted, pieces, left, right):
    cell = lax.broadcasted_iota(jnp.int32, (CELLS, CH), 0)
    for r, piece in enumerate(pieces):
        value = piece.astype(F32)
        shifted[1, r * CELLS : (r + 1) * CELLS, :] = piece.astype(BF)
        plus = jnp.where(cell == CELLS - 1, right[r : r + 1, :], pltpu.roll(value, CELLS - 1, 0))
        minus = jnp.where(cell == 0, left[r : r + 1, :], pltpu.roll(value, 1, 0))
        shifted[2, r * CELLS : (r + 1) * CELLS, :] = plus.astype(BF)
        shifted[0, r * CELLS : (r + 1) * CELLS, :] = minus.astype(BF)


def main_kernel(
    gather,
    offset,
    state,
    outer,
    inner,
    arrived,
    cot,
    conv,
    act_base,
    flux_weight,
    regrid,
    hg_out,
    send_out,
    grads,
    flux_out,
    shifted,
    turned,
    hidden,
):
    ox = lax.axis_index("ox")
    core = lax.axis_index("core")
    left = arrived[lax.rem(ox + NLON - 1, NLON), 32:48, :].astype(F32)
    right = arrived[lax.rem(ox + 1, NLON), 32:48, :].astype(F32)
    top, bottom = halo_rows(outer, inner)
    build_shifts(shifted, [top] + own_rows(state) + [bottom], left, right)
    for half in range(2):
        acc = jnp.zeros((256, CH), F32)
        for t in range(9):
            start = (t // 3) * CELLS + half * 256
            acc = acc + dot(shifted[t % 3, start : start + 256, :], conv[t], ((1,), (0,)))
        hidden[half * 256 : half * 256 + 256, :] = acc
    flux = [
        sum(arrived[s, h * 16 : h * 16 + 16, :].astype(F32) for s in range(NLON)) for h in range(2)
    ]
    blocks = jnp.concatenate(
        [flux[f // 2][:, (f % 2) * 128 : (f % 2) * 128 + 128] for f in range(4)], axis=0
    ).astype(BF)
    contribution = jnp.zeros((64, 128), F32)
    for m in range(8):
        product = dot(blocks, regrid[m], ((1,), (1,)))
        for side in range(2):
            part = product[:, side * 128 : side * 128 + 128]
            contribution = jnp.where(offset[...] == 2 * m + side, part, contribution)
    contribution = contribution.astype(BF)
    cells = dot(gather[...], contribution, ((1,), (0,)))
    cells_high, cells_low = split_two(cells)
    cells_pair = jnp.concatenate([cells_high, cells_low], axis=0)
    pair_row = lax.broadcasted_iota(jnp.int32, (32, CH), 0)
    field_weights = jnp.concatenate([flux_weight[...].astype(F32)] * 8, axis=0)
    flux_part = jnp.zeros((32, CH), F32)
    for r in range(ROWS):
        lo, hi = r * CELLS, (r + 1) * CELLS
        mine = lax.rem(pair_row, 16) // 4 == r
        weights = jnp.where(mine, field_weights, 0.0).astype(BF)
        act_grad = act_base[lo:hi, :] + dot(cells_pair, weights, ((0,), (0,)))
        value = hidden[lo:hi, :]
        gate = jax.nn.sigmoid(value)
        activation = (value * gate).astype(BF)
        grad = (act_grad * gate * (1.0 + value * (1.0 - gate))).astype(BF)
        hg_out[lo:hi, :] = grad
        turned[3, :, lo:hi] = activation.T
        flux_part = flux_part + jnp.where(
            mine, dot(cells_pair, activation, ((1,), (0,))), 0.0
        )
    flux_total = jnp.zeros((4, CH), F32)
    for part in range(8):
        flux_total = flux_total + flux_part[part * 4 : part * 4 + 4]
    flux_high, flux_low = split_two(flux_total)
    flux_rows = jnp.concatenate([flux_high.astype(F32), flux_low.astype(F32)], axis=0)
    for q in range(3):
        turned[q] = shifted[q].T
    for t in range(9):
        start = (t // 3) * CELLS
        product = dot(turned[t % 3, :, start : start + 512], hg_out[...], ((1,), (0,)))
        grads[t * CH : (t + 1) * CH, :] = product
    product = dot(turned[3, :, 0:512], cot[...], ((1,), (0,)))
    grads[9 * CH : 10 * CH, :] = product
    for m in range(16):
        other = pl.multiple_of(m * 160 + 80 - core * 80, 8)
        send_out[m * 80 : m * 80 + 80, :] = grads[pl.ds(other, 80), :].astype(BF)
    flux_out[...] = flux_rows
    send_out[1280:1296, :] = jnp.concatenate(
        [flux_rows, jnp.zeros((8, CH), F32)], axis=0
    ).astype(BF)
    first, last = hg_out[0:CELLS, :], hg_out[3 * CELLS : 4 * CELLS, :]
    send_out[1296:1424, :] = jnp.where(core == 0, last, first)
    outer_row = jnp.where(core == 0, first, last)
    ends = [edge_cells([outer_row], edge) for edge in range(2)]
    send_out[1424:1440, :] = jnp.concatenate(ends + [jnp.zeros((14, CH), F32)], axis=0).astype(BF)


def row_kernel(hg, out):
    core = lax.axis_index("core")
    out[...] = jnp.where(core == 0, hg[0:CELLS, :], hg[3 * CELLS : 4 * CELLS, :])


def merge_kernel(grads, flux_rows, got, hg, out, padded, total, moved):
    ox = lax.axis_index("ox")
    core = lax.axis_index("core")
    for m in range(16):
        lo, hi = m * 80, m * 80 + 80
        mine = pl.multiple_of(m * 160 + core * 80, 8)
        total[lo:hi, :] = grads[pl.ds(mine, 80), :] + got[lo:hi, :].astype(F32)
    for c in range(NLON):
        for z in range(8):
            for yh in range(2):
                m = yh * 8 + z
                to = c * 320 + (z * 2 + yh) * SHARE
                moved[to : to + SHARE, :] = total[m * 80 + c * SHARE : m * 80 + c * SHARE + SHARE, :]
    flux = flux_rows[...] + got[1280:1296, :].astype(F32)[0:8]
    flux_high, flux_low = split_two(flux[0:4] + flux[4:8])
    inside = got[1296:1424, :]
    padded[0:CELLS, :] = inside
    padded[CELLS : 5 * CELLS, :] = hg[...]
    padded[5 * CELLS : 6 * CELLS, :] = inside
    pieces = [inside] + own_rows(hg) + [inside, None, None]
    part = lax.broadcasted_iota(jnp.int32, (8, CH), 0)
    drop = jnp.where(core == 0, 0, ROWS + 1)
    first = jnp.where(part == drop, 0.0, edge_cells(pieces, 0))
    last = jnp.where(part == drop, 0.0, edge_cells(pieces, 1))
    ends = got[1424:1440, :].astype(F32)
    first = jnp.where(part == ROWS + 2, ends[0:1], first)
    last = jnp.where(part == ROWS + 2, ends[1:2], last)
    for c in range(NLON):
        to_right = jnp.where(lax.rem(ox + 1, NLON) == c, 1.0, 0.0)
        to_left = jnp.where(lax.rem(ox + NLON - 1, NLON) == c, 1.0, 0.0)
        halo = last * to_right + first * to_left
        out[c, 0:320, :] = moved[c * 320 : c * 320 + 320, :].astype(BF)
        out[c, 320:336, :] = jnp.concatenate(
            [flux_high.astype(F32), flux_low.astype(F32), halo], axis=0
        ).astype(BF)


def side_cells(arrived):
    ox = lax.axis_index("ox")
    left = arrived[lax.rem(ox + NLON - 1, NLON), 320:336, :].astype(F32)[8:16]
    right = arrived[lax.rem(ox + 1, NLON), 320:336, :].astype(F32)[8:16]
    return left, right


def sum_flux(pieces):
    total = pieces[0]
    for piece in pieces[1:]:
        total = total + piece
    return total[0:4] + total[4:8]


def ox_sum_kernel(got, out):
    for z in range(8):
        piece = got[0, z * 40 : z * 40 + 40, :].astype(F32)
        for s in range(1, NLON):
            piece = piece + got[s, z * 40 : z * 40 + 40, :].astype(F32)
        out[z, 0:40, :] = piece.astype(BF)
    flux = sum_flux([got[s, 320:336, :].astype(F32)[0:8] for s in range(NLON)])
    left, right = side_cells(got)
    ends = jnp.concatenate(
        [flux, left[ROWS + 2 : ROWS + 3], right[ROWS + 2 : ROWS + 3], jnp.zeros((2, CH), F32)],
        axis=0,
    ).astype(BF)
    for z in range(8):
        out[z, 40:48, :] = ends


def z_sum_kernel(got, out):
    piece = got[0].astype(F32)
    for s in range(1, 8):
        piece = piece + got[s].astype(F32)
    high, low = split_two(piece[40:44])
    source = lax.rem(lax.axis_index("z") + jnp.where(lax.axis_index("core") == 0, 7, 1), 8)
    ends = got[source, 32:48, :].astype(F32)[12:14]
    tail = [ends, jnp.zeros((2, CH), F32), high.astype(F32), low.astype(F32)]
    for yh in range(2):
        rows = jnp.concatenate([piece[yh * SHARE : yh * SHARE + SHARE]] + tail, axis=0).astype(BF)
        for e in range(4):
            out[e * 2 + yh] = rows


def last_sum_kernel(got, slabs, conv, _, weight_out, flux_out, out, stage, sems):
    oy = oy_index()
    core = lax.axis_index("core")
    z = lax.axis_index("z")
    yh = lax.axis_index("yh")
    wraps = jnp.where(core == 0, z == 0, z == 7)
    index = lax.axis_index("ens") * 2 + jnp.where(wraps, 1 - yh, yh)
    exists = jnp.where(jnp.logical_or(oy == 0, oy == 31), 0.0, 1.0)
    ends = got[index, 16:32, :].astype(F32)[4:6] * exists
    ends = jnp.concatenate([ends, jnp.zeros((14, CH), F32)], axis=0).astype(BF)
    slab = lax.broadcasted_iota(jnp.int32, (16, CH), 0)
    copies = []
    for side in range(2):
        tap = jnp.where(core == 0, 8, 2) - 2 * side
        added = dot(ends, conv[tap], ((1,), (1,)))[side : side + 1]
        value = slabs[side * 16 : side * 16 + 16, :]
        stage[side] = jnp.where(slab == side * 15, value + added, value).astype(BF)
        to = pl.multiple_of(core * (3 * CELLS) + side * (CELLS - 16), 16)
        copies.append(
            pltpu.make_async_copy(stage.at[side], out.at[pl.ds(to, 16), :], sems.at[side])
        )
        copies[-1].start()
    piece = got[0].astype(F32)
    for s in range(1, 8):
        piece = piece + got[s].astype(F32)
    weight_out[...] = piece[0:SHARE] * SCALE
    flux_out[...] = (piece[24:28] + piece[28:32]) * SCALE
    for copy in copies:
        copy.wait()


def spread_kernel(padded, across, cot, conv, out, shifted):
    oy = oy_index()
    core = lax.axis_index("core")
    exists = jnp.where(jnp.logical_or(oy == 0, oy == 31), 0.0, 1.0)
    inside = padded[0:CELLS, :].astype(F32)
    other = across[...].astype(F32) * exists
    top = jnp.where(core == 0, other, inside)
    bottom = jnp.where(core == 0, inside, other)
    nothing = jnp.zeros((8, CH), F32)
    own = [padded[r * CELLS : (r + 1) * CELLS, :] for r in range(1, ROWS + 1)]
    build_shifts(shifted, [top] + own + [bottom], nothing, nothing)
    for half in range(2):
        acc = cot[half * 256 : half * 256 + 256, :].astype(F32)
        for t in range(9):
            start = (2 - t // 3) * CELLS + half * 256
            acc = acc + dot(shifted[2 - t % 3, start : start + 256, :], conv[t], ((1,), (1,)))
        out[half * 256 : half * 256 + 256, :] = acc


def input_kernel(partial, arrived, conv, out, slabs):
    core = lax.axis_index("core")
    out[...] = partial[...].astype(BF)
    slab = lax.broadcasted_iota(jnp.int32, (16, CH), 0)
    for side, cells in enumerate(side_cells(arrived)):
        cells = jnp.concatenate([cells, jnp.zeros((8, CH), F32)], axis=0).astype(BF)
        added = jnp.zeros((ROWS, CH), F32)
        for p in (-1, 0, 1):
            product = dot(cells, conv[3 * (p + 1) + 2 - 2 * side], ((1,), (1,)))
            added = added + product[1 - p : 1 - p + ROWS]
        values = []
        for r in range(ROWS):
            to = r * CELLS + side * (CELLS - 16)
            value = partial[to : to + 16, :]
            value = jnp.where(slab == side * 15, value + added[r : r + 1], value)
            out[to : to + 16, :] = value.astype(BF)
            values.append(value)
        slabs[side * 16 : side * 16 + 16, :] = jnp.where(core == 0, values[0], values[3])


def body(
    state,
    state_cot,
    flux_cot,
    conv_weight,
    mix_weight,
    flux_weight,
    regrid_weights,
    intersection_atm,
    intersection_offset,
    wet_rows,
):
    state = state.reshape(ROWS * CELLS, CH)
    cot = state_cot.reshape(ROWS * CELLS, CH)
    up, down, state = call(
        first_kernel,
        (
            struct((4 * CELLS, 128), BF),
            struct((4 * CELLS, 128), BF),
            struct((ROWS * CELLS, CH), BF),
        ),
        scratch=[
            pltpu.VMEM((64, 4, 128), BF),
            pltpu.VMEM((256, 128), F32),
            pltpu.SemaphoreType.DMA((2,)),
        ],
        specs=[HBM] * 2,
    )(state, flux_cot.reshape(64, 4, 128))
    outer = lax.ppermute(up, OY, SWAP)
    inner = lax.ppermute(down, "core", [(0, 1), (1, 0)])
    regrid_weights = regrid_weights.reshape(8, 256, 128)
    needed = (cot, conv_weight, mix_weight, flux_weight, regrid_weights)
    pick, offset, gather, act_base, cot, conv_weight, flux_weight, regrid_weights = call(
        pick_kernel,
        (struct((64, 128), BF), struct((64, 128), jnp.int32), struct((16, 64), BF))
        + (struct((ROWS * CELLS, CH), F32),)
        + tuple(struct(a.shape, a.dtype) for a in needed if a is not mix_weight),
        scratch=[
            pltpu.SMEM((4, 4, 128), jnp.int32),
            pltpu.SMEM((4, 4, 128), jnp.int32),
            pltpu.VMEM((CH, CH), BF),
            pltpu.SemaphoreType.DMA((7,)),
        ],
        specs=[HBM] * 2 + [SM] + [HBM] * 5,
    )(
        intersection_atm.transpose(1, 2, 0),
        intersection_offset.transpose(1, 2, 0),
        wet_rows,
        *needed,
    )
    packed = call(pack_kernel, struct((NLON, 48, CH), BF), n_in=5)(pick, state, outer, inner, up)
    arrived = lax.all_to_all(packed, "ox", 0, 0, tiled=True)
    hg, send, grads, flux_rows = call(
        main_kernel,
        (
            struct((ROWS * CELLS, CH), BF),
            struct((1440, CH), BF),
            struct((2560, CH), F32),
            struct((8, CH), F32),
        ),
        scratch=[
            pltpu.VMEM((3, 768, CH), BF),
            pltpu.VMEM((4, CH, 768), BF),
            pltpu.VMEM((512, CH), F32),
        ],
        n_in=11,
    )(gather, offset, state, outer, inner, arrived, cot, conv_weight, act_base, flux_weight, regrid_weights)
    got = lax.ppermute(send, "core", [(0, 1), (1, 0)])
    zrow = call(row_kernel, struct((CELLS, CH), BF), n_in=1)(hg)
    across = lax.ppermute(zrow, OY, SWAP)
    packed, padded = call(
        merge_kernel,
        (struct((NLON, 336, CH), BF), struct((768, CH), BF)),
        scratch=[pltpu.VMEM((1280, CH), F32), pltpu.VMEM((1280, CH), F32)],
        n_in=4,
    )(grads, flux_rows, got, hg)
    by_ox = lax.all_to_all(packed, "ox", 0, 0, tiled=True)
    packed = call(ox_sum_kernel, struct((8, 48, CH), BF), n_in=1)(by_ox)
    by_z = lax.all_to_all(packed, "z", 0, 0, tiled=True)
    packed = call(z_sum_kernel, struct((8, 32, CH), BF), n_in=1)(by_z)
    by_rest = lax.all_to_all(packed, ("ens", "yh"), 0, 0, tiled=True)
    partial = call(
        spread_kernel,
        struct((ROWS * CELLS, CH), F32),
        scratch=[pltpu.VMEM((3, 768, CH), BF)],
        n_in=4,
    )(padded, across, cot, conv_weight)
    plain = jax.ShapeDtypeStruct
    input_grad, slabs = call(
        input_kernel,
        (plain((ROWS * CELLS, CH), BF), struct((32, CH), F32)),
        n_in=3,
    )(partial, by_ox, conv_weight)
    weight_out, flux_out, input_grad = call(
        last_sum_kernel,
        (plain((SHARE, CH), F32), plain((4, CH), F32), plain((ROWS * CELLS, CH), BF)),
        scratch=[pltpu.VMEM((2, 16, CH), BF), pltpu.SemaphoreType.DMA((2,))],
        specs=[VM, VM, VM, HBM],
        outs_at=(VM, VM, HBM),
        aliases={3: 2},
    )(by_rest, slabs, conv_weight, input_grad)
    return (input_grad.reshape(1, ROWS, CELLS, CH), weight_out, flux_out)


def solution(mesh):
    fine = Mesh(mesh.devices.reshape(4, 2, 8, 2, 4), ("ens", "yh", "z", "core", "ox"))
    in_specs = (
        P("ens", OY, "ox", None),
        P("ens", OY, "ox", None),
        P("ens", OY + ("ox",), None, None),
        P(),
        P(),
        P(),
        P(),
        P(),
        P(),
        P(OY, "ox"),
    )
    out_specs = (P("ens", OY, "ox", None), P(OY + ("ox",), None), P())

    return jax.shard_map(body, mesh=fine, in_specs=in_specs, out_specs=out_specs, check_vma=False)
```
